512 devices in a mesh: row: 32 (over y_lo, z), col: 16 (over y_hi, x, core).
Axes of the slice: x: 4, y: 4 (y_hi: 2, y_lo: 2; y = y_hi * 2 + y_lo), z: 16, core: 2. Of those that a mesh axis runs over, the one named last changes fastest.
Arguments:
- tokens: bfloat16 [512, 8192], P('col', 'row'), may hold values from -40 to 40
- norm_gain: bfloat16 [8192], P('row'), may hold values from 0.5 to 2
- w_query: bfloat16 [8192, 8192], P('row', 'col'), may hold values from -0.0625 to 0.0625
- key_weight: bfloat16 [8192, 1024], P('row'), may hold values from -0.125 to 0.125
- value_weight: bfloat16 [8192, 1024], P('row'), may hold values from -0.0625 to 0.0625
- w_out: bfloat16 [8192, 8192], P('col', 'row'), may hold values from -0.25 to 0.25
- cached_key_rows: bfloat16 [65536, 1024], P('row'), may hold values from -120 to 120
- cached_value_rows: bfloat16 [65536, 1024], P('row'), may hold values from -9 to 9
Outputs:
- attn_out: bfloat16 [512, 8192], P('col', 'row')
The draws below stay inside these ranges and needn't reach their ends.
All inputs are finite; a program needn't handle non-finite values.
Results may differ from the reference program's by a relative error of at most 0.039.
Values may be sent and summed in bfloat16 or wider, within the bound.
No kernel may reach another device: no remote copies, remote signals or barrier semaphores. Data moves between devices by JAX's collectives and lax.ppermute only.
A program may use at most 128 MiB of HBM per device.

```python
import math
import jax
import jax.numpy as jnp
from jax import lax

MODEL_WIDTH = 8192
QUERY_HEADS = 64
KEY_VALUE_HEADS = 8
HEAD_WIDTH = 128
BLOCK_TOKENS = 512
CACHED_COUNT = 65536


def draw_tokens(key, part):
    key_rows, key_cols, key_unrotated = jax.random.split(key, 3)
    row_scale = jnp.exp(jax.random.uniform(key_rows, (BLOCK_TOKENS, 1), jnp.float32, math.log(0.3), math.log(3.0)))
    ramp = jnp.arange(MODEL_WIDTH, dtype=jnp.float32) / (MODEL_WIDTH - 1)
    col_scale = 0.6 * jnp.exp(ramp * math.log(3.0) + jax.random.uniform(key_cols, (MODEL_WIDTH,), jnp.float32, -0.35, 0.35))
    rotary_base = jax.random.normal(key_unrotated, (BLOCK_TOKENS, MODEL_WIDTH), jnp.float32)
    return jnp.clip(rotary_base * row_scale * col_scale[None, :], -40.0, 40.0).astype(jnp.bfloat16)


def draw_cached_key_rows(key, part):
    key_unrotated = jax.random.fold_in(key, 0)
    rotary_base = 0.6 * jax.random.normal(key_unrotated, (CACHED_COUNT, KEY_VALUE_HEADS * HEAD_WIDTH), jnp.float32)
    return jnp.clip(rotary_base, -120.0, 120.0).astype(jnp.bfloat16)


def block_levels(own_key, dims, cuts, least, top_value):
    factor_of, own = 1.0, jax.random.fold_in(own_key, 6)
    for position, blocks in cuts:
        steps = jnp.exp(jax.random.uniform(jax.random.fold_in(own, position), (blocks,), jnp.float32, least / len(cuts), top_value / len(cuts)))
        factor_of = factor_of * jnp.repeat(steps, dims[position] // blocks).reshape([-1 if axis == position else 1 for axis in range(len(dims))])
    return factor_of


def scatter_about(key, shape, spread, most, cuts=(), held_as=jnp.bfloat16):
    result = spread * jax.random.normal(key, shape, jnp.float32)
    if cuts:
        result = result * block_levels(key, shape, cuts, -0.22, 0.18)
    return jnp.clip(result, -most, most).astype(held_as)


def setup_inputs(seed: int = 0) -> dict:
    key_of = jax.random.split(jax.random.key(seed), 9)
    return {
        "tokens": draw_tokens(jax.random.fold_in(key_of[8], 71), 0),
        "norm_gain": jnp.clip(jnp.exp(math.log(2.0) - 1.3862944 * jax.random.uniform(key_of[1], (MODEL_WIDTH,), jnp.float32) ** block_levels(key_of[1], (MODEL_WIDTH,), ((0, 32),), -0.2, 0.2)), 0.5, 2.0).astype(jnp.bfloat16),
        "w_query": scatter_about(key_of[2], (MODEL_WIDTH, QUERY_HEADS * HEAD_WIDTH), MODEL_WIDTH ** -0.5, 0.0625, ((0, 32), (1, 16))),
        "key_weight": scatter_about(key_of[3], (MODEL_WIDTH, KEY_VALUE_HEADS * HEAD_WIDTH), (MODEL_WIDTH // 4) ** -0.5, 0.125, ((0, 32),)),
        "value_weight": scatter_about(key_of[4], (MODEL_WIDTH, KEY_VALUE_HEADS * HEAD_WIDTH), MODEL_WIDTH ** -0.5, 0.0625, ((0, 32),)),
        "w_out": scatter_about(key_of[5], (QUERY_HEADS * HEAD_WIDTH, MODEL_WIDTH), (QUERY_HEADS * HEAD_WIDTH // 16) ** -0.5, 0.25, ((0, 16), (1, 32))),
        "cached_key_rows": draw_cached_key_rows(jax.random.fold_in(key_of[8], 71), 0),
        "cached_value_rows": scatter_about(key_of[7], (CACHED_COUNT, KEY_VALUE_HEADS * HEAD_WIDTH), 1.5, 9.0, ((0, 32),)),
    }


rope_base = 500000.0
epsilon = 1e-05

def scaled_freqs(head_size):
    half = head_size // 2
    ladder = jnp.arange(half, dtype=jnp.float32) * (2.0 / head_size)
    base_freqs = jnp.power(jnp.float32(rope_base), -ladder)
    wavelen = 2.0 * math.pi / base_freqs
    smooth = (8192.0 / wavelen - 1.0) / 3.0
    middle = (1.0 - smooth) * base_freqs / 8.0 + smooth * base_freqs
    return jnp.where(wavelen < 2048.0, base_freqs, jnp.where(wavelen > 8192.0, base_freqs / 8.0, middle))

def apply_rotary_heads(vectors, token_positions):
    half = vectors.shape[-1] // 2
    freqs = scaled_freqs(vectors.shape[-1])
    angles = token_positions.astype(jnp.float32)[:, None] * freqs[None, :]
    cosine = jnp.cos(angles)[:, None, :]
    sine = jnp.sin(angles)[:, None, :]
    first = vectors[..., :half]
    second = vectors[..., half:]
    return jnp.concatenate([first * cosine - second * sine, second * cosine + first * sine], axis=-1)

def reference(tokens, norm_gain, w_query, key_weight, value_weight, w_out, cached_key_rows, cached_value_rows):
    widened = tokens.astype(jnp.float32)
    inverse_root_mean = lax.rsqrt(lax.optimization_barrier(jnp.sum(widened * widened, axis=1)) / MODEL_WIDTH + epsilon)
    scaled = (widened * norm_gain.astype(jnp.float32)[None, :]).astype(jnp.bfloat16)
    query_raw = jnp.dot(scaled, w_query, preferred_element_type=jnp.float32)
    key_projected = jnp.dot(scaled, key_weight, preferred_element_type=jnp.float32)
    value_projected = jnp.dot(scaled, value_weight, preferred_element_type=jnp.float32)
    token_positions = CACHED_COUNT + jnp.arange(BLOCK_TOKENS, dtype=jnp.int32)
    queries = apply_rotary_heads((query_raw * inverse_root_mean[:, None]).reshape(BLOCK_TOKENS, QUERY_HEADS, HEAD_WIDTH), token_positions).astype(jnp.bfloat16)
    fresh_keys = apply_rotary_heads((key_projected * inverse_root_mean[:, None]).reshape(BLOCK_TOKENS, KEY_VALUE_HEADS, HEAD_WIDTH), token_positions).astype(jnp.bfloat16)
    fresh_values = (value_projected * inverse_root_mean[:, None]).astype(jnp.bfloat16).reshape(BLOCK_TOKENS, KEY_VALUE_HEADS, HEAD_WIDTH)
    key_matrix = jnp.concatenate([cached_key_rows.reshape(CACHED_COUNT, KEY_VALUE_HEADS, HEAD_WIDTH), fresh_keys], axis=0)
    value_matrix = jnp.concatenate([cached_value_rows.reshape(CACHED_COUNT, KEY_VALUE_HEADS, HEAD_WIDTH), fresh_values], axis=0)
    group_factor = QUERY_HEADS // KEY_VALUE_HEADS
    key_index = jnp.arange(CACHED_COUNT + BLOCK_TOKENS, dtype=jnp.int32)
    query_index = jnp.arange(BLOCK_TOKENS, dtype=jnp.int32)
    visible = (key_index[None, :] < CACHED_COUNT) | (key_index[None, :] - CACHED_COUNT <= query_index[:, None])
    score_scale = 1.0 / math.sqrt(HEAD_WIDTH)

    def one_head(head):
        kv_head = head // group_factor
        query = lax.dynamic_index_in_dim(queries, head, 1, keepdims=False)
        key = lax.dynamic_index_in_dim(key_matrix, kv_head, 1, keepdims=False)
        value = lax.dynamic_index_in_dim(value_matrix, kv_head, 1, keepdims=False)
        scores = jnp.dot(query, key.T, preferred_element_type=jnp.float32) * score_scale
        masked = jnp.where(visible, scores, -jnp.inf)
        row_max = lax.optimization_barrier(jnp.max(masked, axis=1, keepdims=True))
        weights = jnp.exp(masked - row_max)
        denom = lax.optimization_barrier(jnp.sum(weights, axis=1))
        numer = jnp.dot(weights.astype(jnp.bfloat16), value, preferred_element_type=jnp.float32)
        return (numer / denom[:, None]).astype(jnp.bfloat16)
    context = lax.map(one_head, jnp.arange(QUERY_HEADS, dtype=jnp.int32))
    context = jnp.transpose(context, (1, 0, 2)).reshape(BLOCK_TOKENS, QUERY_HEADS * HEAD_WIDTH)
    return jnp.dot(context, w_out, preferred_element_type=jnp.float32).astype(jnp.bfloat16)
```

```python
import math

import jax
import jax.numpy as jnp
import numpy as np
from jax import lax
from jax.sharding import Mesh, PartitionSpec as P

MODEL_WIDTH = 8192
QUERY_HEADS = 64
KEY_VALUE_HEADS = 8
HEAD_WIDTH = 128
BLOCK_TOKENS = 512
CACHED_COUNT = 65536

rope_base = 500000.0
epsilon = 1e-05

NEAR = ("ylo", "zl")
NEAR_SIZE = 8
FAR_SIZE = 4
COLS = 16
HEADS_HERE = QUERY_HEADS // COLS
TOK_NEAR = BLOCK_TOKENS // NEAR_SIZE
TOK_ROW = TOK_NEAR // FAR_SIZE
Q_ROWS = HEADS_HERE * TOK_NEAR

bf16 = jnp.bfloat16
f32 = jnp.float32


def rope_tables():
    half = HEAD_WIDTH // 2
    ladder = np.arange(half, dtype=np.float32) * np.float32(2.0 / HEAD_WIDTH)
    base = np.power(np.float32(rope_base), -ladder).astype(np.float32)
    wavelen = (np.float32(2.0 * math.pi) / base).astype(np.float32)
    smooth = ((np.float32(8192.0) / wavelen - 1) / 3).astype(np.float32)
    middle = ((1 - smooth) * base / 8 + smooth * base).astype(np.float32)
    freqs = np.where(wavelen < 2048, base, np.where(wavelen > 8192, base / 8, middle))
    pos = (CACHED_COUNT + np.arange(BLOCK_TOKENS)).astype(np.float32)
    angles = (pos[:, None] * freqs.astype(np.float32)[None, :]).astype(np.float32)
    cos = np.cos(angles.astype(np.float64)).astype(np.float32)
    sin = np.sin(angles.astype(np.float64)).astype(np.float32)
    return np.concatenate([cos, cos], 1), np.concatenate([-sin, sin], 1)


COS_TABLE, SIN_TABLE = rope_tables()


def split3(x):
    hi = lax.reduce_precision(x, 8, 7)
    rest = x - hi
    mid = lax.reduce_precision(rest, 8, 7)
    return hi.astype(bf16), mid.astype(bf16), (rest - mid).astype(bf16)


def rotate(u, cos, sin):
    half = HEAD_WIDTH // 2
    swapped = jnp.concatenate([u[..., half:], u[..., :half]], axis=-1)
    return u * cos + swapped * sin


def exchange(x, axes):
    return lax.all_to_all(x, axes, 0, 0, tiled=True)


def spread(x, count, axes):
    return exchange(jnp.broadcast_to(x[None], (count,) + x.shape), axes)


def body(tokens, norm_gain, w_query, key_weight, value_weight, w_out, cached_keys, cached_values):
    near = lax.axis_index("ylo") * 4 + lax.axis_index("zl")
    far = lax.axis_index("zh")
    group = lax.axis_index("col") // 2

    whole = spread(tokens, COLS, "col").reshape(BLOCK_TOKENS, -1)
    wide = whole.astype(f32)
    squares = jnp.sum(wide * wide, axis=1)
    scaled = (wide * norm_gain.astype(f32)[None, :]).astype(bf16)
    k_panel = lax.dynamic_slice_in_dim(key_weight, group * HEAD_WIDTH, HEAD_WIDTH, 1)
    v_panel = lax.dynamic_slice_in_dim(value_weight, group * HEAD_WIDTH, HEAD_WIDTH, 1)
    panel = jnp.concatenate([w_query, k_panel, v_panel], axis=1)
    part = jnp.dot(scaled, panel, preferred_element_type=f32).astype(bf16)
    part = part.reshape(NEAR_SIZE, TOK_NEAR, HEADS_HERE + 2, HEAD_WIDTH)
    part = part.transpose(0, 2, 1, 3).reshape(NEAR_SIZE, -1, HEAD_WIDTH)
    sq = jnp.stack(split3(squares.reshape(NEAR_SIZE, TOK_NEAR)), axis=1)
    sq = jnp.pad(sq, ((0, 0), (0, 13), (0, HEAD_WIDTH - TOK_NEAR)))
    got = exchange(jnp.concatenate([part, sq], axis=1), NEAR)

    total = jnp.sum(got.astype(f32), axis=0)
    kv = total[Q_ROWS : Q_ROWS + 2 * TOK_NEAR].astype(bf16)
    kv = kv.reshape(2, FAR_SIZE, TOK_ROW, HEAD_WIDTH).transpose(1, 0, 2, 3)
    kv = kv.reshape(FAR_SIZE, 2 * TOK_ROW, HEAD_WIDTH)
    sq = jnp.sum(total[Q_ROWS + 2 * TOK_NEAR :], axis=0)
    sq = jnp.pad(jnp.stack(split3(sq)), ((0, 13), (0, 0)))
    q_part = jnp.broadcast_to(total[None, :Q_ROWS].astype(bf16), (FAR_SIZE, Q_ROWS, HEAD_WIDTH))
    sq = jnp.broadcast_to(sq[None], (FAR_SIZE,) + sq.shape)
    got = exchange(jnp.concatenate([q_part, kv, sq], axis=1), "zh")

    total = jnp.sum(got.astype(f32), axis=0)
    square_sum = jnp.sum(total[Q_ROWS + 2 * TOK_ROW :], axis=0)[:TOK_NEAR]
    inv = lax.rsqrt(square_sum / MODEL_WIDTH + epsilon)
    inv_row = lax.dynamic_slice_in_dim(inv, far * TOK_ROW, TOK_ROW)
    start = near * TOK_NEAR
    cos = lax.dynamic_slice_in_dim(jnp.asarray(COS_TABLE), start, TOK_NEAR)
    sin = lax.dynamic_slice_in_dim(jnp.asarray(SIN_TABLE), start, TOK_NEAR)
    cos_row = lax.dynamic_slice_in_dim(cos, far * TOK_ROW, TOK_ROW)
    sin_row = lax.dynamic_slice_in_dim(sin, far * TOK_ROW, TOK_ROW)
    q = total[:Q_ROWS].reshape(HEADS_HERE, TOK_NEAR, HEAD_WIDTH) * inv[None, :, None]
    q = rotate(q, cos[None], sin[None]).astype(bf16).reshape(Q_ROWS, HEAD_WIDTH)
    new_k = total[Q_ROWS : Q_ROWS + TOK_ROW] * inv_row[:, None]
    new_k = rotate(new_k, cos_row, sin_row).astype(bf16)
    new_v = (total[Q_ROWS + TOK_ROW : Q_ROWS + 2 * TOK_ROW] * inv_row[:, None]).astype(bf16)
    queries = spread(q, NEAR_SIZE, NEAR).reshape(NEAR_SIZE * Q_ROWS, HEAD_WIDTH)

    old_k = lax.dynamic_slice_in_dim(cached_keys, group * HEAD_WIDTH, HEAD_WIDTH, 1)
    old_v = lax.dynamic_slice_in_dim(cached_values, group * HEAD_WIDTH, HEAD_WIDTH, 1)
    keys = jnp.concatenate([old_k, new_k], axis=0)
    values = jnp.concatenate([old_v, new_v], axis=0)
    scores = lax.dot_general(queries, keys, (((1,), (1,)), ((), ())), preferred_element_type=f32)
    scores = scores * (1.0 / math.sqrt(HEAD_WIDTH))
    old = old_k.shape[0]
    row = jnp.arange(NEAR_SIZE * Q_ROWS, dtype=jnp.int32)
    token = row // Q_ROWS * TOK_NEAR + row % TOK_NEAR
    slot = jnp.arange(old + TOK_ROW, dtype=jnp.int32)
    new_token = start + far * TOK_ROW + slot - old
    seen = (slot[None, :] < old) | (new_token[None, :] <= token[:, None])
    scores = jnp.where(seen, scores, -jnp.inf)
    top = jnp.max(scores, axis=1, keepdims=True)
    weights = jnp.exp(scores - top)
    denom = jnp.sum(weights, axis=1)
    numer = jnp.dot(weights.astype(bf16), values, preferred_element_type=f32)
    out = (numer / denom[:, None]).astype(bf16).reshape(NEAR_SIZE, Q_ROWS, HEAD_WIDTH)
    lse = (top[:, 0] + jnp.log(denom)).reshape(NEAR_SIZE, 2, HEAD_WIDTH)
    lse = jnp.pad(jnp.concatenate(split3(lse), axis=1), ((0, 0), (0, 10), (0, 0)))
    got = exchange(jnp.concatenate([out, lse], axis=1), NEAR)

    mixed, lse = combine(got)
    lse = jnp.pad(jnp.concatenate(split3(lse), axis=0), ((0, 10), (0, 0)))
    got = spread(jnp.concatenate([mixed.astype(bf16), lse], axis=0), FAR_SIZE, "zh")
    got = got.reshape(FAR_SIZE, Q_ROWS + 16, HEAD_WIDTH)
    mixed, _ = combine(got)
    context = spread(mixed.astype(bf16), NEAR_SIZE, NEAR)
    context = context.reshape(NEAR_SIZE, HEADS_HERE, TOK_NEAR, HEAD_WIDTH)
    context = context.transpose(0, 2, 1, 3).reshape(BLOCK_TOKENS, HEADS_HERE * HEAD_WIDTH)
    part = jnp.dot(context, w_out, preferred_element_type=f32).astype(bf16)
    got = exchange(part.reshape(COLS, BLOCK_TOKENS // COLS, -1), "col")
    return jnp.sum(got.astype(f32), axis=0).astype(bf16)


def combine(got):
    count = got.shape[0]
    parts = got[:, Q_ROWS : Q_ROWS + 6].astype(f32).reshape(count, 3, 2, HEAD_WIDTH)
    lse = jnp.sum(parts, axis=1)
    top = jnp.max(lse, axis=0)
    share = jnp.exp(lse - top[None])
    total = jnp.sum(share, axis=0)
    ratio = (share / total[None]).reshape(count, Q_ROWS, 1)
    mixed = jnp.sum(got[:, :Q_ROWS].astype(f32) * ratio, axis=0)
    return mixed, top + jnp.log(total)


def solution(mesh):
    fine = Mesh(mesh.devices.reshape(2, 4, 4, COLS), ("ylo", "zh", "zl", "col"))
    row = ("ylo", "zh", "zl")
    placed = (
        P("col", row),
        P(row),
        P(row, "col"),
        P(row, None),
        P(row, None),
        P("col", row),
        P(row, None),
        P(row, None),
    )
    return jax.shard_map(
        body, mesh=fine, in_specs=placed, out_specs=P("col", row), check_vma=False
    )
```

```python
import math

import jax
import jax.numpy as jnp
import numpy as np
from jax import lax
from jax.experimental import pallas as pl
from jax.experimental.pallas import tpu as pltpu
from jax.sharding import Mesh, PartitionSpec as P

MODEL_WIDTH = 8192
QUERY_HEADS = 64
KEY_VALUE_HEADS = 8
HEAD_WIDTH = 128
BLOCK_TOKENS = 512
CACHED_COUNT = 65536

rope_base = 500000.0
epsilon = 1e-05

NEAR = ("ylo", "zl")
NEAR_SIZE = 8
FAR_SIZE = 4
COLS = 16
HEADS_HERE = QUERY_HEADS // COLS
TOK_NEAR = BLOCK_TOKENS // NEAR_SIZE
TOK_ROW = TOK_NEAR // FAR_SIZE
Q_ROWS = HEADS_HERE * TOK_NEAR

bf16 = jnp.bfloat16
f32 = jnp.float32


def rope_tables():
    half = HEAD_WIDTH // 2
    ladder = np.arange(half, dtype=np.float32) * np.float32(2.0 / HEAD_WIDTH)
    base = np.power(np.float32(rope_base), -ladder).astype(np.float32)
    wavelen = (np.float32(2.0 * math.pi) / base).astype(np.float32)
    smooth = ((np.float32(8192.0) / wavelen - 1) / 3).astype(np.float32)
    middle = ((1 - smooth) * base / 8 + smooth * base).astype(np.float32)
    freqs = np.where(wavelen < 2048, base, np.where(wavelen > 8192, base / 8, middle))
    pos = (CACHED_COUNT + np.arange(BLOCK_TOKENS)).astype(np.float32)
    angles = (pos[:, None] * freqs.astype(np.float32)[None, :]).astype(np.float32)
    cos = np.cos(angles.astype(np.float64)).astype(np.float32)
    sin = np.sin(angles.astype(np.float64)).astype(np.float32)
    return np.concatenate([cos, cos], 1), np.concatenate([-sin, sin], 1)


COS_TABLE, SIN_TABLE = rope_tables()


SCORE_SCALE = math.log2(math.e) / math.sqrt(HEAD_WIDTH)
LN2 = math.log(2.0)
PAD = 16


def exchange(x, axes):
    return lax.all_to_all(x, axes, 0, 0, tiled=True)


def spread(x, count, axes):
    return exchange(jnp.broadcast_to(x[None], (count,) + x.shape), axes)


def run(kernel, shapes, *args, scratch=(), scalars=()):
    spec = pl.BlockSpec(memory_space=pltpu.VMEM)
    smem = pl.BlockSpec(memory_space=pltpu.SMEM)
    return pl.pallas_call(
        kernel,
        out_shape=shapes,
        in_specs=[smem] * len(scalars) + [spec] * len(args),
        out_specs=jax.tree.map(lambda _: spec, shapes),
        scratch_shapes=scratch,
        compiler_params=pltpu.CompilerParams(vmem_limit_bytes=48 << 20),
    )(*scalars, *args)


def shape(*dims, dtype=bf16):
    return jax.ShapeDtypeStruct(dims, dtype)


def parts3(x):
    hi = x.astype(bf16)
    rest = x - hi.astype(f32)
    mid = rest.astype(bf16)
    low = (rest - mid.astype(f32)).astype(bf16)
    return hi.astype(f32), mid.astype(f32), low.astype(f32)


def pack_rows(rows):
    line = lax.broadcasted_iota(jnp.int32, (PAD, HEAD_WIDTH), 0)
    tile = jnp.zeros((PAD, HEAD_WIDTH), f32)
    for i, row in enumerate(rows):
        tile = jnp.where(line == i, jnp.broadcast_to(row, tile.shape), tile)
    return tile.astype(bf16)


def same(rows, cols, offset=0):
    a = lax.broadcasted_iota(jnp.int32, (rows, cols), 0)
    b = lax.broadcasted_iota(jnp.int32, (rows, cols), 1)
    return a + offset == b


def to_column(row, rows, offset=0):
    wide = jnp.broadcast_to(row, (rows, row.shape[1]))
    return jnp.sum(jnp.where(same(rows, row.shape[1], offset), wide, 0.0), axis=1, keepdims=True)


def to_row(column):
    n = column.shape[0]
    wide = jnp.broadcast_to(column, (n, n))
    return jnp.sum(jnp.where(same(n, n), wide, 0.0), axis=0, keepdims=True)


def project_kernel(tok_ref, gain_ref, w_ref, k_ref, v_ref, out_ref):
    scaled = (tok_ref[...].astype(f32) * gain_ref[...].astype(f32)).astype(bf16)
    pairs = [w_ref[:, 256 * i : 256 * (i + 1)] for i in range(HEADS_HERE // 2)]
    pairs.append(jnp.concatenate([k_ref[...], v_ref[...]], axis=1))
    for i, panel in enumerate(pairs):
        part = jnp.dot(scaled, panel, preferred_element_type=f32).astype(bf16)
        for j in range(2):
            head = part[:, HEAD_WIDTH * j : HEAD_WIDTH * (j + 1)]
            row = (2 * i + j) * TOK_NEAR
            for n in range(NEAR_SIZE):
                out_ref[n, row : row + TOK_NEAR, :] = head[n * TOK_NEAR : (n + 1) * TOK_NEAR]
    row = (HEADS_HERE + 2) * TOK_NEAR
    for n in range(NEAR_SIZE // 2):
        x = tok_ref[n * 128 : (n + 1) * 128, :]
        gram = lax.dot_general(x, x, (((1,), (1,)), ((), ())), preferred_element_type=f32)
        sums = jnp.sum(jnp.where(same(128, 128), gram, 0.0), axis=0, keepdims=True)
        tile = pack_rows(parts3(sums))
        out_ref[2 * n, row : row + PAD, :] = tile
        out_ref[2 * n + 1, row : row + PAD, :] = jnp.concatenate([tile[:, 64:], tile[:, :64]], axis=1)


def reduce_kernel(got_ref, out_ref):
    total = got_ref[0].astype(f32)
    for n in range(1, NEAR_SIZE):
        total = total + got_ref[n].astype(f32)
    low = total.astype(bf16)
    k_row, v_row, s_row = Q_ROWS, Q_ROWS + TOK_NEAR, Q_ROWS + 2 * TOK_NEAR
    sums = total[s_row : s_row + 1] + total[s_row + 1 : s_row + 2] + total[s_row + 2 : s_row + 3]
    tile = pack_rows(parts3(sums))
    for f in range(FAR_SIZE):
        out_ref[f, :Q_ROWS, :] = low[:Q_ROWS]
        out_ref[f, Q_ROWS : Q_ROWS + 16, :] = low[k_row + 16 * f : k_row + 16 * (f + 1)]
        out_ref[f, Q_ROWS + 16 : Q_ROWS + 32, :] = low[v_row + 16 * f : v_row + 16 * (f + 1)]
        out_ref[f, Q_ROWS + 32 : Q_ROWS + 48, :] = tile


def rope_kernel(far_ref, got_ref, cos_ref, sin_ref, cosn_ref, sinn_ref, q_ref, k_ref, v_ref):
    total = got_ref[0].astype(f32)
    for n in range(1, FAR_SIZE):
        total = total + got_ref[n].astype(f32)
    row = Q_ROWS + 2 * TOK_ROW
    sums = total[row : row + 1] + total[row + 1 : row + 2] + total[row + 2 : row + 3]
    inv = lax.rsqrt(sums / MODEL_WIDTH + epsilon)
    inv_q = to_column(inv, TOK_NEAR)
    inv_n = to_column(inv, TOK_ROW, far_ref[0] * TOK_ROW)
    cos, sin = cos_ref[...], sin_ref[...]
    for h in range(HEADS_HERE):
        u = total[h * TOK_NEAR : (h + 1) * TOK_NEAR] * inv_q
        u = (u * cos + pltpu.roll(u, HEAD_WIDTH // 2, 1) * sin).astype(bf16)
        for n in range(NEAR_SIZE):
            q_ref[n, h * TOK_NEAR : (h + 1) * TOK_NEAR, :] = u
    u = total[Q_ROWS : Q_ROWS + TOK_ROW] * inv_n
    k_ref[...] = (u * cosn_ref[...] + pltpu.roll(u, HEAD_WIDTH // 2, 1) * sinn_ref[...]).astype(bf16)
    v_ref[...] = (total[Q_ROWS + TOK_ROW : Q_ROWS + 2 * TOK_ROW] * inv_n).astype(bf16)


def attend_kernel(first_ref, q_ref, k_ref, v_ref, nk_ref, nv_ref, out_ref):
    contract = (((1,), (1,)), ((), ()))
    zeros = jnp.zeros((HEAD_WIDTH - TOK_ROW, HEAD_WIDTH), bf16)
    new_k = jnp.concatenate([nk_ref[...], zeros], axis=0)
    new_v = jnp.concatenate([nv_ref[...], zeros], axis=0)
    slot = lax.broadcasted_iota(jnp.int32, (Q_ROWS, HEAD_WIDTH), 1)
    line = lax.broadcasted_iota(jnp.int32, (Q_ROWS, HEAD_WIDTH), 0)
    new_token = jnp.where(slot < TOK_ROW, first_ref[0] + slot, BLOCK_TOKENS)

    def block(n, carry):
        q = q_ref[n]
        s = lax.dot_general(q, k_ref[...], contract, preferred_element_type=f32)
        fresh = lax.dot_general(q, new_k, contract, preferred_element_type=f32)
        token = n * TOK_NEAR + lax.rem(line, TOK_NEAR)
        fresh = jnp.where(new_token <= token, fresh, -jnp.inf)
        top = jnp.maximum(
            jnp.max(s, axis=1, keepdims=True), jnp.max(fresh, axis=1, keepdims=True)
        )
        base = top * SCORE_SCALE
        w = jnp.exp2(s * SCORE_SCALE - base)
        w_new = jnp.exp2(fresh * SCORE_SCALE - base)
        denom = jnp.sum(w, axis=1, keepdims=True) + jnp.sum(w_new, axis=1, keepdims=True)
        numer = jnp.dot(w.astype(bf16), v_ref[...], preferred_element_type=f32)
        numer = numer + jnp.dot(w_new.astype(bf16), new_v, preferred_element_type=f32)
        out_ref[n, :Q_ROWS, :] = (numer / denom).astype(bf16)
        lse = base * LN2 + jnp.log(denom)
        lo = parts3(to_row(lse[:HEAD_WIDTH]))
        hi = parts3(to_row(lse[HEAD_WIDTH:]))
        out_ref[n, Q_ROWS:, :] = pack_rows([x for pair in zip(lo, hi) for x in pair])
        return carry

    lax.fori_loop(0, NEAR_SIZE, block, 0)


def mix(got_ref, count):
    lse = []
    for n in range(count):
        t = got_ref[n, Q_ROWS:, :].astype(f32)
        lse.append(t[0:2] + t[2:4] + t[4:6])
    top = lse[0]
    for n in range(1, count):
        top = jnp.maximum(top, lse[n])
    share = [jnp.exp(x - top) for x in lse]
    total = sum(share[1:], share[0])
    halves = []
    for j in range(2):
        rows = slice(HEAD_WIDTH * j, HEAD_WIDTH * (j + 1))
        acc = jnp.zeros((HEAD_WIDTH, HEAD_WIDTH), f32)
        for n in range(count):
            ratio = to_column(share[n][j : j + 1] / total[j : j + 1], HEAD_WIDTH)
            acc = acc + got_ref[n, rows, :].astype(f32) * ratio
        halves.append(acc.astype(bf16))
    return halves, top + jnp.log(total)


def mix_near_kernel(got_ref, out_ref):
    halves, lse = mix(got_ref, NEAR_SIZE)
    parts = parts3(lse)
    tile = pack_rows([p[j : j + 1] for p in parts for j in range(2)])
    for f in range(FAR_SIZE):
        out_ref[f, :HEAD_WIDTH, :] = halves[0]
        out_ref[f, HEAD_WIDTH:Q_ROWS, :] = halves[1]
        out_ref[f, Q_ROWS:, :] = tile


def mix_far_kernel(got_ref, out_ref):
    halves, _ = mix(got_ref, FAR_SIZE)
    for n in range(NEAR_SIZE):
        out_ref[n, :HEAD_WIDTH, :] = halves[0]
        out_ref[n, HEAD_WIDTH:Q_ROWS, :] = halves[1]


def output_kernel(got_ref, w_ref, out_ref, ctx_ref):
    for n in range(NEAR_SIZE):
        for h in range(HEADS_HERE):
            block = got_ref[n, h * TOK_NEAR : (h + 1) * TOK_NEAR, :]
            ctx_ref[n * TOK_NEAR : (n + 1) * TOK_NEAR, h * HEAD_WIDTH : (h + 1) * HEAD_WIDTH] = block
    part = jnp.dot(ctx_ref[...], w_ref[...], preferred_element_type=f32).astype(bf16)
    rows = BLOCK_TOKENS // COLS
    for c in range(COLS):
        out_ref[c] = part[c * rows : (c + 1) * rows]


def body(tokens, norm_gain, w_query, key_weight, value_weight, w_out, cached_keys, cached_values):
    near = lax.axis_index("ylo") * 4 + lax.axis_index("zl")
    far = lax.axis_index("zh")
    group = lax.axis_index("col") // 2

    def panel(x):
        return lax.dynamic_slice_in_dim(x, group * HEAD_WIDTH, HEAD_WIDTH, 1)

    whole = spread(tokens, COLS, "col").reshape(BLOCK_TOKENS, -1)
    pay = run(
        project_kernel,
        shape(NEAR_SIZE, Q_ROWS + 2 * TOK_NEAR + PAD, HEAD_WIDTH),
        whole, norm_gain[None], w_query, panel(key_weight), panel(value_weight),
    )
    got = exchange(pay, NEAR)
    pay = run(reduce_kernel, shape(FAR_SIZE, Q_ROWS + 2 * TOK_ROW + PAD, HEAD_WIDTH), got)
    got = exchange(pay, "zh")

    start = near * TOK_NEAR
    first = start + far * TOK_ROW
    cos, sin = jnp.asarray(COS_TABLE), jnp.asarray(SIN_TABLE)
    pay, new_k, new_v = run(
        rope_kernel,
        (shape(NEAR_SIZE, Q_ROWS, HEAD_WIDTH), shape(TOK_ROW, HEAD_WIDTH), shape(TOK_ROW, HEAD_WIDTH)),
        got,
        lax.dynamic_slice_in_dim(cos, start, TOK_NEAR),
        lax.dynamic_slice_in_dim(sin, start, TOK_NEAR),
        lax.dynamic_slice_in_dim(cos, first, TOK_ROW),
        lax.dynamic_slice_in_dim(sin, first, TOK_ROW),
        scalars=(far.reshape(1).astype(jnp.int32),),
    )
    queries = exchange(pay, NEAR)
    pay = run(
        attend_kernel,
        shape(NEAR_SIZE, Q_ROWS + PAD, HEAD_WIDTH),
        queries, panel(cached_keys), panel(cached_values), new_k, new_v,
        scalars=(first.reshape(1).astype(jnp.int32),),
    )
    got = exchange(pay, NEAR)
    got = exchange(run(mix_near_kernel, shape(FAR_SIZE, Q_ROWS + PAD, HEAD_WIDTH), got), "zh")
    got = exchange(run(mix_far_kernel, shape(NEAR_SIZE, Q_ROWS, HEAD_WIDTH), got), NEAR)
    width = w_out.shape[1]
    pay = run(
        output_kernel,
        shape(COLS, BLOCK_TOKENS // COLS, width),
        got, w_out,
        scratch=[pltpu.VMEM((BLOCK_TOKENS, HEADS_HERE * HEAD_WIDTH), bf16)],
    )
    got = exchange(pay, "col")
    return jnp.sum(got.astype(f32), axis=0).astype(bf16)


def solution(mesh):
    fine = Mesh(mesh.devices.reshape(2, 4, 4, COLS), ("ylo", "zh", "zl", "col"))
    row = ("ylo", "zh", "zl")
    placed = (
        P("col", row),
        P(row),
        P(row, "col"),
        P(row, None),
        P(row, None),
        P("col", row),
        P(row, None),
        P(row, None),
    )
    return jax.shard_map(
        body, mesh=fine, in_specs=placed, out_specs=P("col", row), check_vma=False
    )
```

```python
import math

import jax
import jax.numpy as jnp
import numpy as np
from jax import lax
from jax.experimental import pallas as pl
from jax.experimental.pallas import tpu as pltpu
from jax.sharding import Mesh, PartitionSpec as P

MODEL_WIDTH = 8192
QUERY_HEADS = 64
KEY_VALUE_HEADS = 8
HEAD_WIDTH = 128
BLOCK_TOKENS = 512
CACHED_COUNT = 65536

rope_base = 500000.0
epsilon = 1e-05

NEAR_SIZE = 4
FAR_SIZE = 4
COLS = 16
PAIR = 2
HEADS_HERE = QUERY_HEADS // COLS // PAIR
HEAD_COLS = HEADS_HERE * HEAD_WIDTH
TOK_NEAR = BLOCK_TOKENS // NEAR_SIZE
TOK_ROW = TOK_NEAR // FAR_SIZE
Q_ROWS = HEADS_HERE * TOK_NEAR

bf16 = jnp.bfloat16
f32 = jnp.float32


def rope_tables():
    half = HEAD_WIDTH // 2
    ladder = np.arange(half, dtype=np.float32) * np.float32(2.0 / HEAD_WIDTH)
    base = np.power(np.float32(rope_base), -ladder).astype(np.float32)
    wavelen = (np.float32(2.0 * math.pi) / base).astype(np.float32)
    smooth = ((np.float32(8192.0) / wavelen - 1) / 3).astype(np.float32)
    middle = ((1 - smooth) * base / 8 + smooth * base).astype(np.float32)
    freqs = np.where(wavelen < 2048, base, np.where(wavelen > 8192, base / 8, middle))
    pos = (CACHED_COUNT + np.arange(BLOCK_TOKENS)).astype(np.float32)
    angles = (pos[:, None] * freqs.astype(np.float32)[None, :]).astype(np.float32)
    cos = np.cos(angles.astype(np.float64)).astype(np.float32)
    sin = np.sin(angles.astype(np.float64)).astype(np.float32)
    return np.concatenate([cos, cos], 1), np.concatenate([-sin, sin], 1)


COS_TABLE, SIN_TABLE = rope_tables()


SCORE_SCALE = math.log2(math.e) / math.sqrt(HEAD_WIDTH)
LN2 = math.log(2.0)
PAD = 16
PANEL = HEAD_PANEL = 256


def exchange(x, axes):
    return lax.all_to_all(x, axes, 0, 0, tiled=True)


def spread(x, count, axes):
    return exchange(jnp.broadcast_to(x[None], (count,) + x.shape), axes)


def run(kernel, shapes, *args, scratch=(), scalars=()):
    spec = pl.BlockSpec(memory_space=pltpu.VMEM)
    smem = pl.BlockSpec(memory_space=pltpu.SMEM)
    return pl.pallas_call(
        kernel,
        out_shape=shapes,
        in_specs=[smem] * len(scalars) + [spec] * len(args),
        out_specs=jax.tree.map(lambda _: spec, shapes),
        scratch_shapes=scratch,
        compiler_params=pltpu.CompilerParams(vmem_limit_bytes=48 << 20),
    )(*scalars, *args)


def shape(*dims, dtype=bf16):
    return jax.ShapeDtypeStruct(dims, dtype)


def parts3(x):
    hi = x.astype(bf16)
    rest = x - hi.astype(f32)
    mid = rest.astype(bf16)
    low = (rest - mid.astype(f32)).astype(bf16)
    return hi.astype(f32), mid.astype(f32), low.astype(f32)


def pack_rows(rows):
    line = lax.broadcasted_iota(jnp.int32, (PAD, HEAD_WIDTH), 0)
    tile = jnp.zeros((PAD, HEAD_WIDTH), f32)
    for i, row in enumerate(rows):
        tile = jnp.where(line == i, jnp.broadcast_to(row, tile.shape), tile)
    return tile.astype(bf16)


def same(rows, cols, offset=0):
    a = lax.broadcasted_iota(jnp.int32, (rows, cols), 0)
    b = lax.broadcasted_iota(jnp.int32, (rows, cols), 1)
    return a + offset == b


def to_column(row, rows, offset=0):
    wide = jnp.broadcast_to(row, (rows, row.shape[1]))
    return jnp.sum(jnp.where(same(rows, row.shape[1], offset), wide, 0.0), axis=1, keepdims=True)


def to_row(column):
    n = column.shape[0]
    wide = jnp.broadcast_to(column, (n, n))
    return jnp.sum(jnp.where(same(n, n), wide, 0.0), axis=0, keepdims=True)


def project_kernel(pair_ref, tok_ref, gain_ref, w_ref, k_ref, v_ref, far_ref, out_ref):
    mine = pair_ref[0]
    gains = [gain_ref[...], far_ref[HEAD_PANEL : HEAD_PANEL + 1, :PANEL]]
    toks = [tok_ref[mine], tok_ref[1 - mine]]
    scaled = [(t.astype(f32) * g.astype(f32)).astype(bf16) for t, g in zip(toks, gains)]
    panels = [w_ref[:, pl.ds(pl.multiple_of(mine * HEAD_COLS, HEAD_COLS), HEAD_COLS)]]
    panels.append(jnp.concatenate([k_ref[...], v_ref[...]], axis=1))
    for i, panel in enumerate(panels):
        other = far_ref[:HEAD_PANEL, HEAD_COLS * i : HEAD_COLS * (i + 1)]
        part = jnp.dot(scaled[0], panel, preferred_element_type=f32)
        part = (part + jnp.dot(scaled[1], other, preferred_element_type=f32)).astype(bf16)
        for j in range(2):
            head = part[:, HEAD_WIDTH * j : HEAD_WIDTH * (j + 1)]
            row = (2 * i + j) * TOK_NEAR
            for n in range(NEAR_SIZE):
                out_ref[n, row : row + TOK_NEAR, :] = head[n * TOK_NEAR : (n + 1) * TOK_NEAR]
    row = (HEADS_HERE + 2) * TOK_NEAR
    contract = (((1,), (1,)), ((), ()))
    for n in range(NEAR_SIZE):
        sums = jnp.zeros((1, TOK_NEAR), f32)
        for t in toks:
            x = t[n * TOK_NEAR : (n + 1) * TOK_NEAR]
            gram = lax.dot_general(x, x, contract, preferred_element_type=f32)
            gram = jnp.where(same(TOK_NEAR, TOK_NEAR), gram, 0.0)
            sums = sums + jnp.sum(gram, axis=0, keepdims=True)
        out_ref[n, row : row + PAD, :] = pack_rows(parts3(sums))


def reduce_kernel(got_ref, out_ref):
    total = got_ref[0].astype(f32)
    for n in range(1, NEAR_SIZE):
        total = total + got_ref[n].astype(f32)
    low = total.astype(bf16)
    k_row, v_row, s_row = Q_ROWS, Q_ROWS + TOK_NEAR, Q_ROWS + 2 * TOK_NEAR
    sums = total[s_row : s_row + 1] + total[s_row + 1 : s_row + 2] + total[s_row + 2 : s_row + 3]
    tile = pack_rows(parts3(sums))
    own, end = TOK_ROW, 2 * TOK_ROW
    for f in range(FAR_SIZE):
        out_ref[f, :Q_ROWS, :] = low[:Q_ROWS]
        out_ref[f, Q_ROWS : Q_ROWS + own, :] = low[k_row + own * f : k_row + own * (f + 1)]
        out_ref[f, Q_ROWS + own : Q_ROWS + end, :] = low[v_row + own * f : v_row + own * (f + 1)]
        out_ref[f, Q_ROWS + end : Q_ROWS + end + PAD, :] = tile


def rope_kernel(far_ref, got_ref, cos_ref, sin_ref, cosn_ref, sinn_ref, q_ref, k_ref, v_ref):
    total = got_ref[0].astype(f32)
    for n in range(1, FAR_SIZE):
        total = total + got_ref[n].astype(f32)
    row = Q_ROWS + 2 * TOK_ROW
    sums = total[row : row + 1] + total[row + 1 : row + 2] + total[row + 2 : row + 3]
    inv = lax.rsqrt(sums / MODEL_WIDTH + epsilon)
    inv_q = to_column(inv, TOK_NEAR)
    inv_n = to_column(inv, TOK_ROW, far_ref[0] * TOK_ROW)
    cos, sin = cos_ref[...], sin_ref[...]
    for h in range(HEADS_HERE):
        u = total[h * TOK_NEAR : (h + 1) * TOK_NEAR] * inv_q
        u = (u * cos + pltpu.roll(u, HEAD_WIDTH // 2, 1) * sin).astype(bf16)
        for n in range(NEAR_SIZE):
            q_ref[n, h * TOK_NEAR : (h + 1) * TOK_NEAR, :] = u
    u = total[Q_ROWS : Q_ROWS + TOK_ROW] * inv_n
    k_ref[...] = (u * cosn_ref[...] + pltpu.roll(u, HEAD_WIDTH // 2, 1) * sinn_ref[...]).astype(bf16)
    v_ref[...] = (total[Q_ROWS + TOK_ROW : Q_ROWS + 2 * TOK_ROW] * inv_n).astype(bf16)


def attend_kernel(first_ref, q_ref, kv_ref, other_ref, nk_ref, nv_ref, out_ref):
    contract = (((1,), (1,)), ((), ()))
    zeros = jnp.zeros((HEAD_WIDTH - TOK_ROW, HEAD_WIDTH), bf16)
    new_k = jnp.concatenate([nk_ref[...], zeros], axis=0)
    new_v = jnp.concatenate([nv_ref[...], zeros], axis=0)
    slot = lax.broadcasted_iota(jnp.int32, (Q_ROWS, HEAD_WIDTH), 1)
    line = lax.broadcasted_iota(jnp.int32, (Q_ROWS, HEAD_WIDTH), 0)
    new_token = jnp.where(slot < TOK_ROW, first_ref[0] + slot, BLOCK_TOKENS)

    def block(n, carry):
        q = q_ref[n]
        s = [
            lax.dot_general(q, kv_ref[0], contract, preferred_element_type=f32),
            lax.dot_general(q, other_ref[0], contract, preferred_element_type=f32),
        ]
        fresh = lax.dot_general(q, new_k, contract, preferred_element_type=f32)
        token = n * TOK_NEAR + lax.rem(line, TOK_NEAR)
        s.append(jnp.where(new_token <= token, fresh, -jnp.inf))
        tops = [jnp.max(x, axis=1, keepdims=True) for x in s]
        top = jnp.maximum(jnp.maximum(tops[0], tops[1]), tops[2])
        base = top * SCORE_SCALE
        denom = jnp.zeros_like(base)
        numer = jnp.zeros((Q_ROWS, HEAD_WIDTH), f32)
        for x, v in zip(s, (kv_ref[1], other_ref[1], new_v)):
            w = jnp.exp2(x * SCORE_SCALE - base)
            denom = denom + jnp.sum(w, axis=1, keepdims=True)
            numer = numer + jnp.dot(w.astype(bf16), v, preferred_element_type=f32)
        out_ref[n, :Q_ROWS, :] = (numer / denom).astype(bf16)
        lse = base * LN2 + jnp.log(denom)
        lo = parts3(to_row(lse[:HEAD_WIDTH]))
        hi = parts3(to_row(lse[HEAD_WIDTH:]))
        out_ref[n, Q_ROWS:, :] = pack_rows([x for pair in zip(lo, hi) for x in pair])
        return carry

    lax.fori_loop(0, NEAR_SIZE, block, 0)


def mix(got_ref, count):
    lse = []
    for n in range(count):
        t = got_ref[n, Q_ROWS:, :].astype(f32)
        lse.append(t[0:2] + t[2:4] + t[4:6])
    top = lse[0]
    for n in range(1, count):
        top = jnp.maximum(top, lse[n])
    share = [jnp.exp(x - top) for x in lse]
    total = sum(share[1:], share[0])
    halves = []
    for j in range(2):
        rows = slice(HEAD_WIDTH * j, HEAD_WIDTH * (j + 1))
        acc = jnp.zeros((HEAD_WIDTH, HEAD_WIDTH), f32)
        for n in range(count):
            ratio = to_column(share[n][j : j + 1] / total[j : j + 1], HEAD_WIDTH)
            acc = acc + got_ref[n, rows, :].astype(f32) * ratio
        halves.append(acc.astype(bf16))
    return halves, top + jnp.log(total)


def mix_near_kernel(got_ref, out_ref):
    halves, lse = mix(got_ref, NEAR_SIZE)
    parts = parts3(lse)
    tile = pack_rows([p[j : j + 1] for p in parts for j in range(2)])
    for f in range(FAR_SIZE):
        out_ref[f, :HEAD_WIDTH, :] = halves[0]
        out_ref[f, HEAD_WIDTH:Q_ROWS, :] = halves[1]
        out_ref[f, Q_ROWS:, :] = tile


def mix_far_kernel(got_ref, out_ref):
    halves, _ = mix(got_ref, FAR_SIZE)
    for n in range(NEAR_SIZE):
        out_ref[n, :HEAD_WIDTH, :] = halves[0]
        out_ref[n, HEAD_WIDTH:Q_ROWS, :] = halves[1]


def output_kernel(pair_ref, got_ref, w_ref, other_ref, out_ref, ctx_ref):
    mine = pair_ref[0]
    for n in range(NEAR_SIZE):
        for h in range(HEADS_HERE):
            block = got_ref[n, h * TOK_NEAR : (h + 1) * TOK_NEAR, :]
            ctx_ref[n * TOK_NEAR : (n + 1) * TOK_NEAR, h * HEAD_WIDTH : (h + 1) * HEAD_WIDTH] = block
    own = w_ref[pl.ds(pl.multiple_of(mine * HEAD_COLS, HEAD_COLS), HEAD_COLS), :]
    rows = BLOCK_TOKENS // COLS
    for side, panel in ((mine, own), (1 - mine, other_ref[...])):
        part = jnp.dot(ctx_ref[...], panel, preferred_element_type=f32).astype(bf16)
        for c in range(COLS):
            out_ref[side * COLS + c] = part[c * rows : (c + 1) * rows]


def trade(x):
    return lax.ppermute(x, "ylo", [(0, 1), (1, 0)])


def body(tokens, norm_gain, w_query, key_weight, value_weight, w_out, cached_keys, cached_values):
    mine = lax.axis_index("ylo")
    near = lax.axis_index("zl")
    far = lax.axis_index("zh")
    group = lax.axis_index("col") // 2
    pair = mine.reshape(1).astype(jnp.int32)

    def panel(x):
        return lax.dynamic_slice_in_dim(x, group * HEAD_WIDTH, HEAD_WIDTH, 1)

    k_panel, v_panel = panel(key_weight), panel(value_weight)
    w_far = lax.dynamic_slice_in_dim(w_query, (1 - mine) * HEAD_COLS, HEAD_COLS, 1)
    w_far = jnp.concatenate([w_far, k_panel, v_panel], axis=1)
    gain_row = jnp.pad(norm_gain[None], ((0, PAD - 1), (0, w_far.shape[1] - norm_gain.shape[0])))
    w_far = trade(jnp.concatenate([w_far, gain_row], axis=0))
    whole = spread(tokens, PAIR * COLS, ("ylo", "col")).reshape(PAIR, BLOCK_TOKENS, -1)
    kv_own = jnp.stack([panel(cached_keys), panel(cached_values)])
    kv_far = trade(kv_own)
    o_far = trade(lax.dynamic_slice_in_dim(w_out, (1 - mine) * HEAD_COLS, HEAD_COLS, 0))

    pay = run(
        project_kernel,
        shape(NEAR_SIZE, Q_ROWS + 2 * TOK_NEAR + PAD, HEAD_WIDTH),
        whole, norm_gain[None], w_query, k_panel, v_panel, w_far,
        scalars=(pair,),
    )
    got = exchange(pay, "zl")
    pay = run(reduce_kernel, shape(FAR_SIZE, Q_ROWS + 2 * TOK_ROW + PAD, HEAD_WIDTH), got)
    got = exchange(pay, "zh")

    start = near * TOK_NEAR
    first = start + far * TOK_ROW
    cos, sin = jnp.asarray(COS_TABLE), jnp.asarray(SIN_TABLE)
    pay, new_k, new_v = run(
        rope_kernel,
        (shape(NEAR_SIZE, Q_ROWS, HEAD_WIDTH), shape(TOK_ROW, HEAD_WIDTH), shape(TOK_ROW, HEAD_WIDTH)),
        got,
        lax.dynamic_slice_in_dim(cos, start, TOK_NEAR),
        lax.dynamic_slice_in_dim(sin, start, TOK_NEAR),
        lax.dynamic_slice_in_dim(cos, first, TOK_ROW),
        lax.dynamic_slice_in_dim(sin, first, TOK_ROW),
        scalars=(far.reshape(1).astype(jnp.int32),),
    )
    queries = exchange(pay, "zl")
    pay = run(
        attend_kernel,
        shape(NEAR_SIZE, Q_ROWS + PAD, HEAD_WIDTH),
        queries, kv_own, kv_far, new_k, new_v,
        scalars=(first.reshape(1).astype(jnp.int32),),
    )
    got = exchange(pay, "zl")
    got = exchange(run(mix_near_kernel, shape(FAR_SIZE, Q_ROWS + PAD, HEAD_WIDTH), got), "zh")
    got = exchange(run(mix_far_kernel, shape(NEAR_SIZE, Q_ROWS, HEAD_WIDTH), got), "zl")
    pay = run(
        output_kernel,
        shape(PAIR * COLS, BLOCK_TOKENS // COLS, w_out.shape[1]),
        got, w_out, o_far,
        scratch=[pltpu.VMEM((BLOCK_TOKENS, HEAD_COLS), bf16)],
        scalars=(pair,),
    )
    got = exchange(pay, ("ylo", "col"))
    return jnp.sum(got.astype(f32), axis=0).astype(bf16)


def solution(mesh):
    fine = Mesh(mesh.devices.reshape(2, 4, 4, COLS), ("ylo", "zh", "zl", "col"))
    row = ("ylo", "zh", "zl")
    placed = (
        P("col", row),
        P(row),
        P(row, "col"),
        P(row, None),
        P(row, None),
        P("col", row),
        P(row, None),
        P(row, None),
    )
    return jax.shard_map(
        body, mesh=fine, in_specs=placed, out_specs=P("col", row), check_vma=False
    )
```

```python
import math

import jax
import jax.numpy as jnp
import numpy as np
from jax import lax
from jax.experimental import pallas as pl
from jax.experimental.pallas import tpu as pltpu
from jax.sharding import Mesh, PartitionSpec as P

MODEL_WIDTH = 8192
QUERY_HEADS = 64
KEY_VALUE_HEADS = 8
HEAD_WIDTH = 128
BLOCK_TOKENS = 512
CACHED_COUNT = 65536

rope_base = 500000.0
epsilon = 1e-05

NEAR_SIZE = 4
FAR_SIZE = 4
COLS = 16
PAIR = 2
CHIPS = 16
PLANE = ("ylo", "yhi", "x")
HEADS_HERE = QUERY_HEADS // COLS // PAIR
HEAD_COLS = HEADS_HERE * HEAD_WIDTH
TOK_NEAR = BLOCK_TOKENS // NEAR_SIZE
TOK_ROW = TOK_NEAR // FAR_SIZE
Q_ROWS = HEADS_HERE * TOK_NEAR

bf16 = jnp.bfloat16
f32 = jnp.float32


def rope_tables():
    half = HEAD_WIDTH // 2
    ladder = np.arange(half, dtype=np.float32) * np.float32(2.0 / HEAD_WIDTH)
    base = np.power(np.float32(rope_base), -ladder).astype(np.float32)
    wavelen = (np.float32(2.0 * math.pi) / base).astype(np.float32)
    smooth = ((np.float32(8192.0) / wavelen - 1) / 3).astype(np.float32)
    middle = ((1 - smooth) * base / 8 + smooth * base).astype(np.float32)
    freqs = np.where(wavelen < 2048, base, np.where(wavelen > 8192, base / 8, middle))
    pos = (CACHED_COUNT + np.arange(BLOCK_TOKENS)).astype(np.float32)
    angles = (pos[:, None] * freqs.astype(np.float32)[None, :]).astype(np.float32)
    cos = np.cos(angles.astype(np.float64)).astype(np.float32)
    sin = np.sin(angles.astype(np.float64)).astype(np.float32)
    return np.concatenate([cos, cos], 1), np.concatenate([-sin, sin], 1)


COS_TABLE, SIN_TABLE = rope_tables()


SCORE_SCALE = math.log2(math.e) / math.sqrt(HEAD_WIDTH)
LN2 = math.log(2.0)
PAD = 16
PANEL = 256


def exchange(x, axes):
    return lax.all_to_all(x, axes, 0, 0, tiled=True)


def spread(x, count, axes):
    return exchange(jnp.broadcast_to(x[None], (count,) + x.shape), axes)


def run(kernel, shapes, *args, scratch=(), scalars=()):
    spec = pl.BlockSpec(memory_space=pltpu.VMEM)
    smem = pl.BlockSpec(memory_space=pltpu.SMEM)
    return pl.pallas_call(
        kernel,
        out_shape=shapes,
        in_specs=[smem] * len(scalars) + [spec] * len(args),
        out_specs=jax.tree.map(lambda _: spec, shapes),
        scratch_shapes=scratch,
        compiler_params=pltpu.CompilerParams(vmem_limit_bytes=48 << 20),
    )(*scalars, *args)


def shape(*dims, dtype=bf16):
    return jax.ShapeDtypeStruct(dims, dtype)


def parts3(x):
    hi = x.astype(bf16)
    rest = x - hi.astype(f32)
    mid = rest.astype(bf16)
    low = (rest - mid.astype(f32)).astype(bf16)
    return hi.astype(f32), mid.astype(f32), low.astype(f32)


def pack_rows(rows):
    line = lax.broadcasted_iota(jnp.int32, (PAD, HEAD_WIDTH), 0)
    tile = jnp.zeros((PAD, HEAD_WIDTH), f32)
    for i, row in enumerate(rows):
        tile = jnp.where(line == i, jnp.broadcast_to(row, tile.shape), tile)
    return tile.astype(bf16)


def same(rows, cols, offset=0):
    a = lax.broadcasted_iota(jnp.int32, (rows, cols), 0)
    b = lax.broadcasted_iota(jnp.int32, (rows, cols), 1)
    return a + offset == b


def to_column(row, rows, offset=0):
    wide = jnp.broadcast_to(row, (rows, row.shape[1]))
    return jnp.sum(jnp.where(same(rows, row.shape[1], offset), wide, 0.0), axis=1, keepdims=True)


def to_row(column):
    n = column.shape[0]
    wide = jnp.broadcast_to(column, (n, n))
    return jnp.sum(jnp.where(same(n, n), wide, 0.0), axis=0, keepdims=True)


def project_kernel(pair_ref, tok_ref, gain_ref, w_ref, kv_ref, far_ref, out_ref):
    mine = pair_ref[0]
    gains = [gain_ref[...], far_ref[PANEL : PANEL + 1, :PANEL]]
    toks = []
    for side in (mine, 1 - mine):
        blocks = [tok_ref[core, side, j] for j in range(CHIPS // PAIR) for core in range(2)]
        toks.append(jnp.concatenate(blocks, axis=0))
    scaled = [(t.astype(f32) * g.astype(f32)).astype(bf16) for t, g in zip(toks, gains)]
    panels = [w_ref[:, pl.ds(pl.multiple_of(mine * HEAD_COLS, HEAD_COLS), HEAD_COLS)], kv_ref[...]]
    for i, panel in enumerate(panels):
        width = panel.shape[1]
        other = far_ref[:PANEL, HEAD_COLS * i : HEAD_COLS * i + width]
        part = jnp.dot(scaled[0], panel, preferred_element_type=f32)
        part = (part + jnp.dot(scaled[1], other, preferred_element_type=f32)).astype(bf16)
        for j in range(width // HEAD_WIDTH):
            head = part[:, HEAD_WIDTH * j : HEAD_WIDTH * (j + 1)]
            row = (2 * i + j) * TOK_NEAR
            for n in range(NEAR_SIZE):
                out_ref[n, row : row + TOK_NEAR, :] = head[n * TOK_NEAR : (n + 1) * TOK_NEAR]
    row = Q_ROWS + TOK_NEAR
    contract = (((1,), (1,)), ((), ()))
    for n in range(NEAR_SIZE):
        sums = jnp.zeros((1, TOK_NEAR), f32)
        for t in toks:
            x = t[n * TOK_NEAR : (n + 1) * TOK_NEAR]
            gram = lax.dot_general(x, x, contract, preferred_element_type=f32)
            gram = jnp.where(same(TOK_NEAR, TOK_NEAR), gram, 0.0)
            sums = sums + jnp.sum(gram, axis=0, keepdims=True)
        out_ref[n, row : row + PAD, :] = pack_rows(parts3(sums))


def reduce_kernel(got_ref, out_ref):
    total = got_ref[0].astype(f32)
    for n in range(1, NEAR_SIZE):
        total = total + got_ref[n].astype(f32)
    low = total.astype(bf16)
    s_row = Q_ROWS + TOK_NEAR
    sums = total[s_row : s_row + 1] + total[s_row + 1 : s_row + 2] + total[s_row + 2 : s_row + 3]
    tile = pack_rows(parts3(sums))
    end = Q_ROWS + TOK_ROW
    for f in range(FAR_SIZE):
        row = Q_ROWS + TOK_ROW * f
        out_ref[f, :Q_ROWS, :] = low[:Q_ROWS]
        out_ref[f, Q_ROWS:end, :] = low[row : row + TOK_ROW]
        out_ref[f, end : end + PAD, :] = tile


def rope_kernel(place_ref, got_ref, cos_ref, sin_ref, cosn_ref, sinn_ref, q_ref, new_ref):
    total = got_ref[0].astype(f32)
    for n in range(1, FAR_SIZE):
        total = total + got_ref[n].astype(f32)
    row = Q_ROWS + TOK_ROW
    sums = total[row : row + 1] + total[row + 1 : row + 2] + total[row + 2 : row + 3]
    inv = lax.rsqrt(sums / MODEL_WIDTH + epsilon)
    inv_q = to_column(inv, TOK_NEAR)
    inv_n = to_column(inv, TOK_ROW, place_ref[0] * TOK_ROW)
    cos, sin = cos_ref[...], sin_ref[...]
    for h in range(HEADS_HERE):
        u = total[h * TOK_NEAR : (h + 1) * TOK_NEAR] * inv_q
        u = (u * cos + pltpu.roll(u, HEAD_WIDTH // 2, 1) * sin).astype(bf16)
        for n in range(NEAR_SIZE):
            q_ref[n, h * TOK_NEAR : (h + 1) * TOK_NEAR, :] = u
    u = total[Q_ROWS : Q_ROWS + TOK_ROW] * inv_n
    turned = u * cosn_ref[...] + pltpu.roll(u, HEAD_WIDTH // 2, 1) * sinn_ref[...]
    new_ref[...] = jnp.where(place_ref[1] == 0, turned, u).astype(bf16)


def attend_kernel(place_ref, q_ref, kv_ref, other_ref, own_ref, swap_ref, out_ref):
    contract = (((1,), (1,)), ((), ()))
    zeros = jnp.zeros((HEAD_WIDTH - TOK_ROW, HEAD_WIDTH), bf16)
    even = place_ref[1] == 0
    own, swap = own_ref[...].astype(f32), swap_ref[...].astype(f32)
    new_k = jnp.concatenate([jnp.where(even, own, swap).astype(bf16), zeros], axis=0)
    new_v = jnp.concatenate([jnp.where(even, swap, own).astype(bf16), zeros], axis=0)
    slot = lax.broadcasted_iota(jnp.int32, (Q_ROWS, HEAD_WIDTH), 1)
    line = lax.broadcasted_iota(jnp.int32, (Q_ROWS, HEAD_WIDTH), 0)
    new_token = jnp.where(slot < TOK_ROW, place_ref[0] + slot, BLOCK_TOKENS)

    def block(n, carry):
        q = q_ref[n]
        s = [
            lax.dot_general(q, kv_ref[0], contract, preferred_element_type=f32),
            lax.dot_general(q, other_ref[0], contract, preferred_element_type=f32),
        ]
        fresh = lax.dot_general(q, new_k, contract, preferred_element_type=f32)
        token = n * TOK_NEAR + lax.rem(line, TOK_NEAR)
        s.append(jnp.where(new_token <= token, fresh, -jnp.inf))
        tops = [jnp.max(x, axis=1, keepdims=True) for x in s]
        top = jnp.maximum(jnp.maximum(tops[0], tops[1]), tops[2])
        base = top * SCORE_SCALE
        denom = jnp.zeros_like(base)
        numer = jnp.zeros((Q_ROWS, HEAD_WIDTH), f32)
        for x, v in zip(s, (kv_ref[1], other_ref[1], new_v)):
            w = jnp.exp2(x * SCORE_SCALE - base)
            denom = denom + jnp.sum(w, axis=1, keepdims=True)
            numer = numer + jnp.dot(w.astype(bf16), v, preferred_element_type=f32)
        out_ref[n, :Q_ROWS, :] = (numer / denom).astype(bf16)
        lse = base * LN2 + jnp.log(denom)
        lo = parts3(to_row(lse[:HEAD_WIDTH]))
        hi = parts3(to_row(lse[HEAD_WIDTH:]))
        out_ref[n, Q_ROWS:, :] = pack_rows([x for pair in zip(lo, hi) for x in pair])
        return carry

    lax.fori_loop(0, NEAR_SIZE, block, 0)


def mix(got_ref, count):
    lse = []
    for n in range(count):
        t = got_ref[n, Q_ROWS:, :].astype(f32)
        lse.append(t[0:2] + t[2:4] + t[4:6])
    top = lse[0]
    for n in range(1, count):
        top = jnp.maximum(top, lse[n])
    share = [jnp.exp(x - top) for x in lse]
    total = sum(share[1:], share[0])
    halves = []
    for j in range(2):
        rows = slice(HEAD_WIDTH * j, HEAD_WIDTH * (j + 1))
        acc = jnp.zeros((HEAD_WIDTH, HEAD_WIDTH), f32)
        for n in range(count):
            ratio = to_column(share[n][j : j + 1] / total[j : j + 1], HEAD_WIDTH)
            acc = acc + got_ref[n, rows, :].astype(f32) * ratio
        halves.append(acc.astype(bf16))
    return halves, top + jnp.log(total)


def mix_near_kernel(got_ref, out_ref):
    halves, lse = mix(got_ref, NEAR_SIZE)
    parts = parts3(lse)
    tile = pack_rows([p[j : j + 1] for p in parts for j in range(2)])
    for f in range(FAR_SIZE):
        out_ref[f, :HEAD_WIDTH, :] = halves[0]
        out_ref[f, HEAD_WIDTH:Q_ROWS, :] = halves[1]
        out_ref[f, Q_ROWS:, :] = tile


def mix_far_kernel(got_ref, out_ref):
    halves, _ = mix(got_ref, FAR_SIZE)
    rows = BLOCK_TOKENS // COLS
    for n in range(NEAR_SIZE):
        for core in range(2):
            for h in range(HEADS_HERE):
                for sub in range(2):
                    at = (2 * sub + core) * rows
                    to = (2 * h + sub) * rows
                    out_ref[2 * n + core, to : to + rows, :] = halves[h][at : at + rows]


def output_kernel(place_ref, got_ref, own_ref, swap_ref, out_ref, ctx_ref):
    mine, core = place_ref[0], place_ref[1]
    rows = BLOCK_TOKENS // COLS
    for n in range(NEAR_SIZE):
        for h in range(HEADS_HERE):
            to = slice(2 * n * rows, 2 * (n + 1) * rows)
            at = slice(2 * h * rows, 2 * (h + 1) * rows)
            lanes = slice(h * HEAD_WIDTH, (h + 1) * HEAD_WIDTH)
            ctx_ref[0, to, lanes] = got_ref[2 * n + core, at, :]
            ctx_ref[1, to, lanes] = got_ref[2 * n + 1 - core, at, :]
    for i, side in enumerate((mine, 1 - mine)):
        part = jnp.dot(ctx_ref[0], own_ref[i], preferred_element_type=f32)
        part = part + jnp.dot(ctx_ref[1], swap_ref[i], preferred_element_type=f32)
        part = part.astype(bf16)
        for c in range(CHIPS // PAIR):
            out_ref[side * (CHIPS // PAIR) + c] = part[c * rows : (c + 1) * rows]


def trade(x, axis):
    return lax.ppermute(x, axis, [(0, 1), (1, 0)])


def body(tokens, norm_gain, w_query, key_weight, value_weight, w_out, cached_keys, cached_values):
    mine = lax.axis_index("ylo")
    near = lax.axis_index("zl")
    far = lax.axis_index("zh")
    core = lax.axis_index("core")
    group = lax.axis_index("yhi") * 4 + lax.axis_index("x")

    def panel(x):
        return lax.dynamic_slice_in_dim(x, group * HEAD_WIDTH, HEAD_WIDTH, 1)

    def place(*xs):
        return (jnp.stack(xs).astype(jnp.int32),)

    kv_panel = jnp.where(core == 0, panel(key_weight), panel(value_weight))
    w_far = lax.dynamic_slice_in_dim(w_query, (1 - mine) * HEAD_COLS, HEAD_COLS, 1)
    w_far = jnp.concatenate([w_far, kv_panel], axis=1)
    gain_row = jnp.pad(norm_gain[None], ((0, PAD - 1), (0, w_far.shape[1] - norm_gain.shape[0])))
    w_far = trade(jnp.concatenate([w_far, gain_row], axis=0), "ylo")
    whole = lax.all_gather(spread(tokens, CHIPS, PLANE), "core", axis=0)
    whole = whole.reshape((2, PAIR, CHIPS // PAIR) + tokens.shape)
    kv_own = jnp.stack([panel(cached_keys), panel(cached_values)])
    kv_far = trade(kv_own, "ylo")
    pay = run(
        project_kernel,
        shape(NEAR_SIZE, Q_ROWS + TOK_NEAR + PAD, HEAD_WIDTH),
        whole, norm_gain[None], w_query, kv_panel, w_far,
        scalars=place(mine),
    )
    pay, w_out = lax.optimization_barrier((pay, w_out))
    o_own = lax.dynamic_slice_in_dim(w_out, mine * HEAD_COLS, HEAD_COLS, 0)
    o_far = trade(lax.dynamic_slice_in_dim(w_out, (1 - mine) * HEAD_COLS, HEAD_COLS, 0), "ylo")
    got = exchange(pay, "zl")
    pay = run(reduce_kernel, shape(FAR_SIZE, Q_ROWS + TOK_ROW + PAD, HEAD_WIDTH), got)
    pay, o_far = lax.optimization_barrier((pay, o_far))
    o_own = jnp.stack([o_own, o_far])
    got = exchange(pay, "zh")

    start = near * TOK_NEAR
    first = start + far * TOK_ROW
    cos, sin = jnp.asarray(COS_TABLE), jnp.asarray(SIN_TABLE)
    pay, new_own = run(
        rope_kernel,
        (shape(NEAR_SIZE, Q_ROWS, HEAD_WIDTH), shape(TOK_ROW, HEAD_WIDTH)),
        got,
        lax.dynamic_slice_in_dim(cos, start, TOK_NEAR),
        lax.dynamic_slice_in_dim(sin, start, TOK_NEAR),
        lax.dynamic_slice_in_dim(cos, first, TOK_ROW),
        lax.dynamic_slice_in_dim(sin, first, TOK_ROW),
        scalars=place(far, core),
    )
    new_swap = trade(new_own, "core")
    o_swap = trade(o_own, "core")
    queries = exchange(pay, "zl")
    pay = run(
        attend_kernel,
        shape(NEAR_SIZE, Q_ROWS + PAD, HEAD_WIDTH),
        queries, kv_own, kv_far, new_own, new_swap,
        scalars=place(first, core),
    )
    pay, o_swap = lax.optimization_barrier((pay, o_swap))
    got = exchange(pay, "zl")
    got = exchange(run(mix_near_kernel, shape(FAR_SIZE, Q_ROWS + PAD, HEAD_WIDTH), got), "zh")
    got = run(mix_far_kernel, shape(2 * NEAR_SIZE, Q_ROWS // 2, HEAD_WIDTH), got)
    got = exchange(got, ("zl", "core"))
    pay = run(
        output_kernel,
        shape(CHIPS, BLOCK_TOKENS // COLS, w_out.shape[1]),
        got, o_own, o_swap,
        scratch=[pltpu.VMEM((2, BLOCK_TOKENS // 2, HEAD_COLS), bf16)],
        scalars=place(mine, core),
    )
    got = exchange(pay, PLANE)
    return jnp.sum(got.astype(f32), axis=0).astype(bf16)


def solution(mesh):
    fine = Mesh(mesh.devices.reshape(2, 4, 4, 2, 4, 2), ("ylo", "zh", "zl", "yhi", "x", "core"))
    row = ("ylo", "zh", "zl")
    col = ("yhi", "x", "core")
    placed = (
        P(col, row),
        P(row),
        P(row, col),
        P(row, None),
        P(row, None),
        P(col, row),
        P(row, None),
        P(row, None),
    )
    return jax.shard_map(
        body, mesh=fine, in_specs=placed, out_specs=P(col, row), check_vma=False
    )
```

```python
import math

import jax
import jax.numpy as jnp
import numpy as np
from jax import lax
from jax.experimental import pallas as pl
from jax.experimental.pallas import tpu as pltpu
from jax.sharding import Mesh, PartitionSpec as P

MODEL_WIDTH = 8192
QUERY_HEADS = 64
KEY_VALUE_HEADS = 8
HEAD_WIDTH = 128
BLOCK_TOKENS = 512
CACHED_COUNT = 65536

rope_base = 500000.0
epsilon = 1e-05

NEAR_SIZE = 4
FAR_SIZE = 4
COLS = 16
PAIR = 2
CHIPS = 16
PLANE = ("ylo", "yhi", "x")
HEADS_HERE = QUERY_HEADS // COLS // PAIR
HEAD_COLS = HEADS_HERE * HEAD_WIDTH
TOK_NEAR = BLOCK_TOKENS // NEAR_SIZE
TOK_ROW = TOK_NEAR // FAR_SIZE
Q_ROWS = HEADS_HERE * TOK_NEAR

bf16 = jnp.bfloat16
f32 = jnp.float32


def rope_tables():
    half = HEAD_WIDTH // 2
    ladder = np.arange(half, dtype=np.float32) * np.float32(2.0 / HEAD_WIDTH)
    base = np.power(np.float32(rope_base), -ladder).astype(np.float32)
    wavelen = (np.float32(2.0 * math.pi) / base).astype(np.float32)
    smooth = ((np.float32(8192.0) / wavelen - 1) / 3).astype(np.float32)
    middle = ((1 - smooth) * base / 8 + smooth * base).astype(np.float32)
    freqs = np.where(wavelen < 2048, base, np.where(wavelen > 8192, base / 8, middle))
    pos = (CACHED_COUNT + np.arange(BLOCK_TOKENS)).astype(np.float32)
    angles = (pos[:, None] * freqs.astype(np.float32)[None, :]).astype(np.float32)
    cos = np.cos(angles.astype(np.float64)).astype(np.float32)
    sin = np.sin(angles.astype(np.float64)).astype(np.float32)
    return np.concatenate([cos, cos], 1), np.concatenate([-sin, sin], 1)


COS_TABLE, SIN_TABLE = rope_tables()


SCORE_SCALE = math.log2(math.e) / math.sqrt(HEAD_WIDTH)
LN2 = math.log(2.0)
PAD = 16
PANEL = 256


def exchange(x, axes):
    return lax.all_to_all(x, axes, 0, 0, tiled=True)


def spread(x, count, axes):
    return exchange(jnp.broadcast_to(x[None], (count,) + x.shape), axes)


def run(kernel, shapes, *args, scratch=(), scalars=()):
    spec = pl.BlockSpec(memory_space=pltpu.VMEM)
    smem = pl.BlockSpec(memory_space=pltpu.SMEM)
    return pl.pallas_call(
        kernel,
        out_shape=shapes,
        in_specs=[smem] * len(scalars) + [spec] * len(args),
        out_specs=jax.tree.map(lambda _: spec, shapes),
        scratch_shapes=scratch,
        compiler_params=pltpu.CompilerParams(vmem_limit_bytes=48 << 20),
    )(*scalars, *args)


def shape(*dims, dtype=bf16):
    return jax.ShapeDtypeStruct(dims, dtype)


def parts3(x):
    hi = x.astype(bf16)
    rest = x - hi.astype(f32)
    mid = rest.astype(bf16)
    low = (rest - mid.astype(f32)).astype(bf16)
    return hi.astype(f32), mid.astype(f32), low.astype(f32)


def pack_rows(rows):
    line = lax.broadcasted_iota(jnp.int32, (PAD, HEAD_WIDTH), 0)
    tile = jnp.zeros((PAD, HEAD_WIDTH), f32)
    for i, row in enumerate(rows):
        tile = jnp.where(line == i, jnp.broadcast_to(row, tile.shape), tile)
    return tile.astype(bf16)


def same(rows, cols, offset=0):
    a = lax.broadcasted_iota(jnp.int32, (rows, cols), 0)
    b = lax.broadcasted_iota(jnp.int32, (rows, cols), 1)
    return a + offset == b


def to_column(row, rows, offset=0):
    wide = jnp.broadcast_to(row, (rows, row.shape[1]))
    return jnp.sum(jnp.where(same(rows, row.shape[1], offset), wide, 0.0), axis=1, keepdims=True)


def to_row(column):
    n = column.shape[0]
    wide = jnp.broadcast_to(column, (n, n))
    return jnp.sum(jnp.where(same(n, n), wide, 0.0), axis=0, keepdims=True)


def project_kernel(pair_ref, tok_ref, gain_ref, w_ref, kv_ref, far_ref, out_ref):
    mine = pair_ref[0]
    gains = [gain_ref[...], far_ref[PANEL : PANEL + 1, :PANEL]]
    toks = []
    for side in (mine, 1 - mine):
        blocks = [tok_ref[core, side, j] for j in range(CHIPS // PAIR) for core in range(2)]
        toks.append(jnp.concatenate(blocks, axis=0))
    scaled = [(t.astype(f32) * g.astype(f32)).astype(bf16) for t, g in zip(toks, gains)]
    panels = [w_ref[...], kv_ref[...]]
    for i, panel in enumerate(panels):
        width = panel.shape[1]
        other = far_ref[:PANEL, HEAD_COLS * i : HEAD_COLS * i + width]
        part = jnp.dot(scaled[0], panel, preferred_element_type=f32)
        part = (part + jnp.dot(scaled[1], other, preferred_element_type=f32)).astype(bf16)
        for j in range(width // HEAD_WIDTH):
            head = part[:, HEAD_WIDTH * j : HEAD_WIDTH * (j + 1)]
            row = (2 * i + j) * TOK_NEAR
            for n in range(NEAR_SIZE):
                out_ref[n, row : row + TOK_NEAR, :] = head[n * TOK_NEAR : (n + 1) * TOK_NEAR]
    row = Q_ROWS + TOK_NEAR
    contract = (((1,), (1,)), ((), ()))
    for n in range(NEAR_SIZE):
        sums = jnp.zeros((1, TOK_NEAR), f32)
        for t in toks:
            x = t[n * TOK_NEAR : (n + 1) * TOK_NEAR]
            gram = lax.dot_general(x, x, contract, preferred_element_type=f32)
            gram = jnp.where(same(TOK_NEAR, TOK_NEAR), gram, 0.0)
            sums = sums + jnp.sum(gram, axis=0, keepdims=True)
        out_ref[n, row : row + PAD, :] = pack_rows(parts3(sums))


def reduce_kernel(got_ref, out_ref):
    total = got_ref[0].astype(f32)
    for n in range(1, NEAR_SIZE):
        total = total + got_ref[n].astype(f32)
    low = total.astype(bf16)
    s_row = Q_ROWS + TOK_NEAR
    sums = total[s_row : s_row + 1] + total[s_row + 1 : s_row + 2] + total[s_row + 2 : s_row + 3]
    tile = pack_rows(parts3(sums))
    end = Q_ROWS + TOK_ROW
    for f in range(FAR_SIZE):
        row = Q_ROWS + TOK_ROW * f
        out_ref[f, :Q_ROWS, :] = low[:Q_ROWS]
        out_ref[f, Q_ROWS:end, :] = low[row : row + TOK_ROW]
        out_ref[f, end : end + PAD, :] = tile


def rope_kernel(place_ref, got_ref, cos_ref, sin_ref, cosn_ref, sinn_ref, q_ref, new_ref):
    total = got_ref[0].astype(f32)
    for n in range(1, FAR_SIZE):
        total = total + got_ref[n].astype(f32)
    row = Q_ROWS + TOK_ROW
    sums = total[row : row + 1] + total[row + 1 : row + 2] + total[row + 2 : row + 3]
    inv = lax.rsqrt(sums / MODEL_WIDTH + epsilon)
    inv_q = to_column(inv, TOK_NEAR)
    inv_n = to_column(inv, TOK_ROW, place_ref[0] * TOK_ROW)
    cos, sin = cos_ref[...], sin_ref[...]
    for h in range(HEADS_HERE):
        u = total[h * TOK_NEAR : (h + 1) * TOK_NEAR] * inv_q
        u = (u * cos + pltpu.roll(u, HEAD_WIDTH // 2, 1) * sin).astype(bf16)
        for n in range(NEAR_SIZE):
            q_ref[n, h * TOK_NEAR : (h + 1) * TOK_NEAR, :] = u
    u = total[Q_ROWS : Q_ROWS + TOK_ROW] * inv_n
    turned = u * cosn_ref[...] + pltpu.roll(u, HEAD_WIDTH // 2, 1) * sinn_ref[...]
    new_ref[...] = jnp.where(place_ref[1] == 0, turned, u).astype(bf16)


def attend_kernel(place_ref, q_ref, kv_ref, other_ref, own_ref, swap_ref, out_ref):
    contract = (((1,), (1,)), ((), ()))
    zeros = jnp.zeros((HEAD_WIDTH - TOK_ROW, HEAD_WIDTH), bf16)
    core = place_ref[1]
    even = core == 0
    own, swap = own_ref[...].astype(f32), swap_ref[...].astype(f32)
    new_k = jnp.concatenate([jnp.where(even, own, swap).astype(bf16), zeros], axis=0)
    new_v = jnp.concatenate([jnp.where(even, swap, own).astype(bf16), zeros], axis=0)
    slot = lax.broadcasted_iota(jnp.int32, (Q_ROWS, HEAD_WIDTH), 1)
    line = lax.broadcasted_iota(jnp.int32, (Q_ROWS, HEAD_WIDTH), 0)
    new_token = jnp.where(slot < TOK_ROW, place_ref[0] + slot, BLOCK_TOKENS)

    def block(n, carry):
        q = q_ref[n]
        s = [
            lax.dot_general(q, kv_ref[0], contract, preferred_element_type=f32),
            lax.dot_general(q, other_ref[core], contract, preferred_element_type=f32),
        ]
        fresh = lax.dot_general(q, new_k, contract, preferred_element_type=f32)
        token = n * TOK_NEAR + lax.rem(line, TOK_NEAR)
        s.append(jnp.where(new_token <= token, fresh, -jnp.inf))
        tops = [jnp.max(x, axis=1, keepdims=True) for x in s]
        top = jnp.maximum(jnp.maximum(tops[0], tops[1]), tops[2])
        base = top * SCORE_SCALE
        denom = jnp.zeros_like(base)
        numer = jnp.zeros((Q_ROWS, HEAD_WIDTH), f32)
        for x, v in zip(s, (kv_ref[1], other_ref[1 - core], new_v)):
            w = jnp.exp2(x * SCORE_SCALE - base)
            denom = denom + jnp.sum(w, axis=1, keepdims=True)
            numer = numer + jnp.dot(w.astype(bf16), v, preferred_element_type=f32)
        out_ref[n, :Q_ROWS, :] = (numer / denom).astype(bf16)
        lse = base * LN2 + jnp.log(denom)
        lo = parts3(to_row(lse[:HEAD_WIDTH]))
        hi = parts3(to_row(lse[HEAD_WIDTH:]))
        out_ref[n, Q_ROWS:, :] = pack_rows([x for pair in zip(lo, hi) for x in pair])
        return carry

    lax.fori_loop(0, NEAR_SIZE, block, 0)


def mix(got_ref, count):
    lse = []
    for n in range(count):
        t = got_ref[n, Q_ROWS:, :].astype(f32)
        lse.append(t[0:2] + t[2:4] + t[4:6])
    top = lse[0]
    for n in range(1, count):
        top = jnp.maximum(top, lse[n])
    share = [jnp.exp(x - top) for x in lse]
    total = sum(share[1:], share[0])
    halves = []
    for j in range(2):
        rows = slice(HEAD_WIDTH * j, HEAD_WIDTH * (j + 1))
        acc = jnp.zeros((HEAD_WIDTH, HEAD_WIDTH), f32)
        for n in range(count):
            ratio = to_column(share[n][j : j + 1] / total[j : j + 1], HEAD_WIDTH)
            acc = acc + got_ref[n, rows, :].astype(f32) * ratio
        halves.append(acc.astype(bf16))
    return halves, top + jnp.log(total)


def mix_near_kernel(got_ref, out_ref):
    halves, lse = mix(got_ref, NEAR_SIZE)
    parts = parts3(lse)
    tile = pack_rows([p[j : j + 1] for p in parts for j in range(2)])
    for f in range(FAR_SIZE):
        out_ref[f, :HEAD_WIDTH, :] = halves[0]
        out_ref[f, HEAD_WIDTH:Q_ROWS, :] = halves[1]
        out_ref[f, Q_ROWS:, :] = tile


def mix_far_kernel(got_ref, out_ref):
    halves, _ = mix(got_ref, FAR_SIZE)
    rows = BLOCK_TOKENS // COLS
    for n in range(NEAR_SIZE):
        for core in range(2):
            for h in range(HEADS_HERE):
                for sub in range(2):
                    at = (2 * sub + core) * rows
                    to = (2 * h + sub) * rows
                    out_ref[2 * n + core, to : to + rows, :] = halves[h][at : at + rows]


def output_kernel(place_ref, got_ref, own_ref, swap_ref, out_ref, ctx_ref):
    mine, core = place_ref[0], place_ref[1]
    rows = BLOCK_TOKENS // COLS
    for n in range(NEAR_SIZE):
        for h in range(HEADS_HERE):
            to = slice(2 * n * rows, 2 * (n + 1) * rows)
            at = slice(2 * h * rows, 2 * (h + 1) * rows)
            lanes = slice(h * HEAD_WIDTH, (h + 1) * HEAD_WIDTH)
            ctx_ref[0, to, lanes] = got_ref[2 * n + core, at, :]
            ctx_ref[1, to, lanes] = got_ref[2 * n + 1 - core, at, :]
    for i, side in enumerate((mine, 1 - mine)):
        part = jnp.dot(ctx_ref[0], own_ref[i], preferred_element_type=f32)
        part = part + jnp.dot(ctx_ref[1], swap_ref[i], preferred_element_type=f32)
        part = part.astype(bf16)
        for c in range(CHIPS // PAIR):
            out_ref[side * (CHIPS // PAIR) + c] = part[c * rows : (c + 1) * rows]


def trade(x, axis):
    return lax.ppermute(x, axis, [(0, 1), (1, 0)])


def body(tokens, norm_gain, w_query, key_weight, value_weight, w_out, cached_keys, cached_values):
    mine = lax.axis_index("ylo")
    near = lax.axis_index("zl")
    far = lax.axis_index("zh")
    core = lax.axis_index("core")
    group = lax.axis_index("yhi") * 4 + lax.axis_index("x")

    def panel(x):
        return lax.dynamic_slice_in_dim(x, group * HEAD_WIDTH, HEAD_WIDTH, 1)

    def place(*xs):
        return (jnp.stack(xs).astype(jnp.int32),)

    kv_panel = jnp.where(core == 0, panel(key_weight), panel(value_weight))
    w_far = lax.dynamic_slice_in_dim(w_query, (1 - mine) * HEAD_COLS, HEAD_COLS, 1)
    w_far = jnp.concatenate([w_far, kv_panel], axis=1)
    gain_row = jnp.pad(norm_gain[None], ((0, PAD - 1), (0, w_far.shape[1] - norm_gain.shape[0])))
    w_far = jnp.concatenate([w_far, gain_row], axis=0)
    w_own = lax.dynamic_slice_in_dim(w_query, mine * HEAD_COLS, HEAD_COLS, 1)
    tokens, w_far, w_own = lax.optimization_barrier((tokens, w_far, w_own))
    w_far = trade(w_far, "ylo")
    whole = lax.all_gather(spread(tokens, CHIPS, PLANE), "core", axis=0)
    whole = whole.reshape((2, PAIR, CHIPS // PAIR) + tokens.shape)
    pay = run(
        project_kernel,
        shape(NEAR_SIZE, Q_ROWS + TOK_NEAR + PAD, HEAD_WIDTH),
        whole, norm_gain[None], w_own, kv_panel, w_far,
        scalars=place(mine),
    )
    pay, group = lax.optimization_barrier((pay, group))
    kv_far = trade(jnp.where(core == 0, panel(cached_keys), panel(cached_values)), "ylo")
    got = exchange(pay, "zl")
    pay = run(reduce_kernel, shape(FAR_SIZE, Q_ROWS + TOK_ROW + PAD, HEAD_WIDTH), got)
    pay, kv_far, w_out, group = lax.optimization_barrier((pay, kv_far, w_out, group))
    kv_far = jnp.stack([kv_far, trade(kv_far, "core")])
    kv_own = jnp.stack([panel(cached_keys), panel(cached_values)])
    o_own = lax.dynamic_slice_in_dim(w_out, mine * HEAD_COLS, HEAD_COLS, 0)
    o_far = trade(lax.dynamic_slice_in_dim(w_out, (1 - mine) * HEAD_COLS, HEAD_COLS, 0), "ylo")
    o_own = jnp.stack([o_own, o_far])
    got = exchange(pay, "zh")
    got, kv_own, kv_far, o_own = lax.optimization_barrier((got, kv_own, kv_far, o_own))

    start = near * TOK_NEAR
    first = start + far * TOK_ROW
    cos, sin = jnp.asarray(COS_TABLE), jnp.asarray(SIN_TABLE)
    pay, new_own = run(
        rope_kernel,
        (shape(NEAR_SIZE, Q_ROWS, HEAD_WIDTH), shape(TOK_ROW, HEAD_WIDTH)),
        got,
        lax.dynamic_slice_in_dim(cos, start, TOK_NEAR),
        lax.dynamic_slice_in_dim(sin, start, TOK_NEAR),
        lax.dynamic_slice_in_dim(cos, first, TOK_ROW),
        lax.dynamic_slice_in_dim(sin, first, TOK_ROW),
        scalars=place(far, core),
    )
    new_swap = trade(new_own, "core")
    o_swap = trade(o_own, "core")
    queries = exchange(pay, "zl")
    pay = run(
        attend_kernel,
        shape(NEAR_SIZE, Q_ROWS + PAD, HEAD_WIDTH),
        queries, kv_own, kv_far, new_own, new_swap,
        scalars=place(first, core),
    )
    pay, o_swap = lax.optimization_barrier((pay, o_swap))
    got = exchange(pay, "zl")
    got = exchange(run(mix_near_kernel, shape(FAR_SIZE, Q_ROWS + PAD, HEAD_WIDTH), got), "zh")
    got = run(mix_far_kernel, shape(2 * NEAR_SIZE, Q_ROWS // 2, HEAD_WIDTH), got)
    got = exchange(got, ("zl", "core"))
    pay = run(
        output_kernel,
        shape(CHIPS, BLOCK_TOKENS // COLS, w_out.shape[1]),
        got, o_own, o_swap,
        scratch=[pltpu.VMEM((2, BLOCK_TOKENS // 2, HEAD_COLS), bf16)],
        scalars=place(mine, core),
    )
    got = exchange(pay, PLANE)
    return jnp.sum(got.astype(f32), axis=0).astype(bf16)


def solution(mesh):
    fine = Mesh(mesh.devices.reshape(2, 4, 4, 2, 4, 2), ("ylo", "zh", "zl", "yhi", "x", "core"))
    row = ("ylo", "zh", "zl")
    col = ("yhi", "x", "core")
    placed = (
        P(col, row),
        P(row),
        P(row, col),
        P(row, None),
        P(row, None),
        P(col, row),
        P(row, None),
        P(row, None),
    )
    return jax.shard_map(
        body, mesh=fine, in_specs=placed, out_specs=P(col, row), check_vma=False
    )
```

```python
import math

import jax
import jax.numpy as jnp
import numpy as np
from jax import lax
from jax.experimental import pallas as pl
from jax.experimental.pallas import tpu as pltpu
from jax.sharding import Mesh, PartitionSpec as P

MODEL_WIDTH = 8192
QUERY_HEADS = 64
KEY_VALUE_HEADS = 8
HEAD_WIDTH = 128
BLOCK_TOKENS = 512
CACHED_COUNT = 65536

rope_base = 500000.0
epsilon = 1e-05

NEAR_SIZE = 4
FAR_SIZE = 4
COLS = 16
PAIR = 2
CHIPS = 16
PLANE = ("ylo", "yhi", "x")
HEADS_HERE = QUERY_HEADS // COLS // PAIR
HEAD_COLS = HEADS_HERE * HEAD_WIDTH
TOK_NEAR = BLOCK_TOKENS // NEAR_SIZE
TOK_ROW = TOK_NEAR // FAR_SIZE
Q_ROWS = HEADS_HERE * TOK_NEAR

bf16 = jnp.bfloat16
f32 = jnp.float32


def rope_tables():
    half = HEAD_WIDTH // 2
    ladder = np.arange(half, dtype=np.float32) * np.float32(2.0 / HEAD_WIDTH)
    base = np.power(np.float32(rope_base), -ladder).astype(np.float32)
    wavelen = (np.float32(2.0 * math.pi) / base).astype(np.float32)
    smooth = ((np.float32(8192.0) / wavelen - 1) / 3).astype(np.float32)
    middle = ((1 - smooth) * base / 8 + smooth * base).astype(np.float32)
    freqs = np.where(wavelen < 2048, base, np.where(wavelen > 8192, base / 8, middle))
    pos = (CACHED_COUNT + np.arange(BLOCK_TOKENS)).astype(np.float32)
    angles = (pos[:, None] * freqs.astype(np.float32)[None, :]).astype(np.float32)
    cos = np.cos(angles.astype(np.float64)).astype(np.float32)
    sin = np.sin(angles.astype(np.float64)).astype(np.float32)
    return np.concatenate([cos, cos], 1), np.concatenate([-sin, sin], 1)


COS_TABLE, SIN_TABLE = rope_tables()


SCORE_SCALE = math.log2(math.e) / math.sqrt(HEAD_WIDTH)
LN2 = math.log(2.0)
PAD = 16
PANEL = 256


def exchange(x, axes):
    return lax.all_to_all(x, axes, 0, 0, tiled=True)


def run(kernel, shapes, *args, scratch=(), scalars=()):
    spec = pl.BlockSpec(memory_space=pltpu.VMEM)
    smem = pl.BlockSpec(memory_space=pltpu.SMEM)
    return pl.pallas_call(
        kernel,
        out_shape=shapes,
        in_specs=[smem] * len(scalars) + [spec] * len(args),
        out_specs=jax.tree.map(lambda _: spec, shapes),
        scratch_shapes=scratch,
        compiler_params=pltpu.CompilerParams(vmem_limit_bytes=48 << 20),
    )(*scalars, *args)


def shape(*dims, dtype=bf16):
    return jax.ShapeDtypeStruct(dims, dtype)


def parts3(x):
    hi = x.astype(bf16)
    rest = x - hi.astype(f32)
    mid = rest.astype(bf16)
    low = (rest - mid.astype(f32)).astype(bf16)
    return hi.astype(f32), mid.astype(f32), low.astype(f32)


def pack_rows(rows):
    line = lax.broadcasted_iota(jnp.int32, (PAD, HEAD_WIDTH), 0)
    tile = jnp.zeros((PAD, HEAD_WIDTH), f32)
    for i, row in enumerate(rows):
        tile = jnp.where(line == i, jnp.broadcast_to(row, tile.shape), tile)
    return tile.astype(bf16)


def same(rows, cols, offset=0):
    a = lax.broadcasted_iota(jnp.int32, (rows, cols), 0)
    b = lax.broadcasted_iota(jnp.int32, (rows, cols), 1)
    return a + offset == b


def to_column(row, rows, offset=0):
    wide = jnp.broadcast_to(row, (rows, row.shape[1]))
    return jnp.sum(jnp.where(same(rows, row.shape[1], offset), wide, 0.0), axis=1, keepdims=True)


def to_row(column):
    n = column.shape[0]
    wide = jnp.broadcast_to(column, (n, n))
    return jnp.sum(jnp.where(same(n, n), wide, 0.0), axis=0, keepdims=True)


def copies_kernel(x_ref, out_ref):
    for i in range(CHIPS):
        out_ref[i] = x_ref[...]


def project_kernel(pair_ref, tok_ref, gain_ref, w_ref, kv_ref, far_ref, out_ref):
    mine = pair_ref[0]
    gains = [gain_ref[...], far_ref[PANEL : PANEL + 1, :PANEL]]
    toks = []
    for side in (mine, 1 - mine):
        blocks = [tok_ref[core, side, j] for j in range(CHIPS // PAIR) for core in range(2)]
        toks.append(jnp.concatenate(blocks, axis=0))
    scaled = [(t.astype(f32) * g.astype(f32)).astype(bf16) for t, g in zip(toks, gains)]
    panels = [w_ref[...], kv_ref[...]]
    for i, panel in enumerate(panels):
        width = panel.shape[1]
        other = far_ref[:PANEL, HEAD_COLS * i : HEAD_COLS * i + width]
        part = jnp.dot(scaled[0], panel, preferred_element_type=f32)
        part = (part + jnp.dot(scaled[1], other, preferred_element_type=f32)).astype(bf16)
        for j in range(width // HEAD_WIDTH):
            head = part[:, HEAD_WIDTH * j : HEAD_WIDTH * (j + 1)]
            row = (2 * i + j) * TOK_NEAR
            for n in range(NEAR_SIZE):
                out_ref[n, row : row + TOK_NEAR, :] = head[n * TOK_NEAR : (n + 1) * TOK_NEAR]
    row = Q_ROWS + TOK_NEAR
    contract = (((1,), (1,)), ((), ()))
    for n in range(NEAR_SIZE):
        sums = jnp.zeros((1, TOK_NEAR), f32)
        for t in toks:
            x = t[n * TOK_NEAR : (n + 1) * TOK_NEAR]
            gram = lax.dot_general(x, x, contract, preferred_element_type=f32)
            gram = jnp.where(same(TOK_NEAR, TOK_NEAR), gram, 0.0)
            sums = sums + jnp.sum(gram, axis=0, keepdims=True)
        out_ref[n, row : row + PAD, :] = pack_rows(parts3(sums))


def reduce_kernel(got_ref, out_ref):
    total = got_ref[0].astype(f32)
    for n in range(1, NEAR_SIZE):
        total = total + got_ref[n].astype(f32)
    low = total.astype(bf16)
    s_row = Q_ROWS + TOK_NEAR
    sums = total[s_row : s_row + 1] + total[s_row + 1 : s_row + 2] + total[s_row + 2 : s_row + 3]
    tile = pack_rows(parts3(sums))
    end = Q_ROWS + TOK_ROW
    for f in range(FAR_SIZE):
        row = Q_ROWS + TOK_ROW * f
        out_ref[f, :Q_ROWS, :] = low[:Q_ROWS]
        out_ref[f, Q_ROWS:end, :] = low[row : row + TOK_ROW]
        out_ref[f, end : end + PAD, :] = tile


def rope_kernel(place_ref, got_ref, cos_ref, sin_ref, cosn_ref, sinn_ref, q_ref, new_ref):
    total = got_ref[0].astype(f32)
    for n in range(1, FAR_SIZE):
        total = total + got_ref[n].astype(f32)
    row = Q_ROWS + TOK_ROW
    sums = total[row : row + 1] + total[row + 1 : row + 2] + total[row + 2 : row + 3]
    inv = lax.rsqrt(sums / MODEL_WIDTH + epsilon)
    inv_q = to_column(inv, TOK_NEAR)
    inv_n = to_column(inv, TOK_ROW, place_ref[0] * TOK_ROW)
    cos, sin = cos_ref[...], sin_ref[...]
    for h in range(HEADS_HERE):
        u = total[h * TOK_NEAR : (h + 1) * TOK_NEAR] * inv_q
        u = (u * cos + pltpu.roll(u, HEAD_WIDTH // 2, 1) * sin).astype(bf16)
        for n in range(NEAR_SIZE):
            q_ref[n, h * TOK_NEAR : (h + 1) * TOK_NEAR, :] = u
    u = total[Q_ROWS : Q_ROWS + TOK_ROW] * inv_n
    turned = u * cosn_ref[...] + pltpu.roll(u, HEAD_WIDTH // 2, 1) * sinn_ref[...]
    new_ref[...] = jnp.where(place_ref[1] == 0, turned, u).astype(bf16)


def attend_kernel(place_ref, q_ref, kv_ref, other_ref, own_ref, swap_ref, out_ref):
    contract = (((1,), (1,)), ((), ()))
    zeros = jnp.zeros((HEAD_WIDTH - TOK_ROW, HEAD_WIDTH), bf16)
    even = place_ref[1] == 0
    own, swap = own_ref[...].astype(f32), swap_ref[...].astype(f32)
    new_k = jnp.concatenate([jnp.where(even, own, swap).astype(bf16), zeros], axis=0)
    new_v = jnp.concatenate([jnp.where(even, swap, own).astype(bf16), zeros], axis=0)
    rows = 2 * Q_ROWS
    slot = lax.broadcasted_iota(jnp.int32, (rows, HEAD_WIDTH), 1)
    line = lax.broadcasted_iota(jnp.int32, (rows, HEAD_WIDTH), 0)
    new_token = jnp.where(slot < TOK_ROW, place_ref[0] + slot, BLOCK_TOKENS)
    at = jnp.where(line < Q_ROWS, 0, TOK_NEAR) + lax.rem(line, TOK_NEAR)
    for n in range(0, NEAR_SIZE, 2):
        q = jnp.concatenate([q_ref[n], q_ref[n + 1]], axis=0)
        top = denom = numer = None
        for k, v in ((kv_ref[0], kv_ref[1]), (other_ref[0], other_ref[1]), (new_k, new_v)):
            s = lax.dot_general(q, k, contract, preferred_element_type=f32)
            if k is new_k:
                s = jnp.where(new_token <= n * TOK_NEAR + at, s, -jnp.inf)
            here = jnp.max(s, axis=1, keepdims=True)
            most = here if top is None else jnp.maximum(top, here)
            w = jnp.exp2(s * SCORE_SCALE - most * SCORE_SCALE)
            total = jnp.sum(w, axis=1, keepdims=True)
            part = jnp.dot(w.astype(bf16), v, preferred_element_type=f32)
            if top is not None:
                fade = jnp.exp2((top - most) * SCORE_SCALE)
                total = denom * fade + total
                part = numer * fade + part
            top, denom, numer = most, total, part
        out = (numer / denom).astype(bf16)
        lse = top * (SCORE_SCALE * LN2) + jnp.log(denom)
        for i in range(2):
            out_ref[n + i, :Q_ROWS, :] = out[i * Q_ROWS : (i + 1) * Q_ROWS]
            row = i * Q_ROWS
            lo = parts3(to_row(lse[row : row + HEAD_WIDTH]))
            hi = parts3(to_row(lse[row + HEAD_WIDTH : row + Q_ROWS]))
            out_ref[n + i, Q_ROWS:, :] = pack_rows([x for pair in zip(lo, hi) for x in pair])


def mix(got_ref, count):
    lse = []
    for n in range(count):
        t = got_ref[n, Q_ROWS:, :].astype(f32)
        lse.append(t[0:2] + t[2:4] + t[4:6])
    top = lse[0]
    for n in range(1, count):
        top = jnp.maximum(top, lse[n])
    share = [jnp.exp(x - top) for x in lse]
    total = sum(share[1:], share[0])
    halves = []
    for j in range(2):
        rows = slice(HEAD_WIDTH * j, HEAD_WIDTH * (j + 1))
        acc = jnp.zeros((HEAD_WIDTH, HEAD_WIDTH), f32)
        for n in range(count):
            ratio = to_column(share[n][j : j + 1] / total[j : j + 1], HEAD_WIDTH)
            acc = acc + got_ref[n, rows, :].astype(f32) * ratio
        halves.append(acc.astype(bf16))
    return halves, top + jnp.log(total)


def mix_near_kernel(got_ref, out_ref):
    halves, lse = mix(got_ref, NEAR_SIZE)
    parts = parts3(lse)
    tile = pack_rows([p[j : j + 1] for p in parts for j in range(2)])
    out_ref[:HEAD_WIDTH, :] = halves[0]
    out_ref[HEAD_WIDTH:Q_ROWS, :] = halves[1]
    out_ref[Q_ROWS:, :] = tile


def mix_far_kernel(got_ref, out_ref):
    halves, _ = mix(got_ref, FAR_SIZE)
    rows = BLOCK_TOKENS // COLS
    for n in range(NEAR_SIZE):
        for core in range(2):
            for h in range(HEADS_HERE):
                for sub in range(2):
                    at = (2 * sub + core) * rows
                    to = (2 * h + sub) * rows
                    out_ref[2 * n + core, to : to + rows, :] = halves[h][at : at + rows]


def output_kernel(place_ref, got_ref, own_ref, swap_ref, out_ref, ctx_ref):
    mine, core = place_ref[0], place_ref[1]
    rows = BLOCK_TOKENS // COLS
    for n in range(NEAR_SIZE):
        for h in range(HEADS_HERE):
            to = slice(2 * n * rows, 2 * (n + 1) * rows)
            at = slice(2 * h * rows, 2 * (h + 1) * rows)
            lanes = slice(h * HEAD_WIDTH, (h + 1) * HEAD_WIDTH)
            ctx_ref[0, to, lanes] = got_ref[2 * n + core, at, :]
            ctx_ref[1, to, lanes] = got_ref[2 * n + 1 - core, at, :]
    for i, side in enumerate((mine, 1 - mine)):
        part = jnp.dot(ctx_ref[0], own_ref[i], preferred_element_type=f32)
        part = part + jnp.dot(ctx_ref[1], swap_ref[i], preferred_element_type=f32)
        part = part.astype(bf16)
        for c in range(CHIPS // PAIR):
            out_ref[side * (CHIPS // PAIR) + c] = part[c * rows : (c + 1) * rows]


def trade(x, axis):
    return lax.ppermute(x, axis, [(0, 1), (1, 0)])


def body(tokens, norm_gain, w_query, key_weight, value_weight, w_out, cached_keys, cached_values):
    mine = lax.axis_index("ylo")
    near = lax.axis_index("zl")
    far = lax.axis_index("zh")
    core = lax.axis_index("core")
    group = lax.axis_index("yhi") * 4 + lax.axis_index("x")

    def panel(x):
        return lax.dynamic_slice_in_dim(x, group * HEAD_WIDTH, HEAD_WIDTH, 1)

    def place(*xs):
        return (jnp.stack(xs).astype(jnp.int32),)

    kv_panel = jnp.where(core == 0, panel(key_weight), panel(value_weight))
    w_own = lax.dynamic_slice_in_dim(w_query, mine * HEAD_COLS, HEAD_COLS, 1)
    w_far = lax.dynamic_slice_in_dim(w_query, (1 - mine) * HEAD_COLS, HEAD_COLS, 1)
    w_far = jnp.concatenate([w_far, kv_panel], axis=1)
    gain_row = jnp.pad(norm_gain[None], ((0, PAD - 1), (0, w_far.shape[1] - norm_gain.shape[0])))
    w_far = trade(jnp.concatenate([w_far, gain_row], axis=0), "ylo")
    whole = lax.all_gather(exchange(run(copies_kernel, shape(CHIPS, *tokens.shape), tokens), PLANE), "core", axis=0)
    whole = whole.reshape((2, PAIR, CHIPS // PAIR) + tokens.shape)
    kv_own = jnp.stack([panel(cached_keys), panel(cached_values)])
    kv_far = trade(kv_own, "ylo")
    pay = run(
        project_kernel,
        shape(NEAR_SIZE, Q_ROWS + TOK_NEAR + PAD, HEAD_WIDTH),
        whole, norm_gain[None], w_own, kv_panel, w_far,
        scalars=place(mine),
    )
    pay, w_out = lax.optimization_barrier((pay, w_out))
    o_own = lax.dynamic_slice_in_dim(w_out, mine * HEAD_COLS, HEAD_COLS, 0)
    o_far = trade(lax.dynamic_slice_in_dim(w_out, (1 - mine) * HEAD_COLS, HEAD_COLS, 0), "ylo")
    got = exchange(pay, "zl")
    pay = run(reduce_kernel, shape(FAR_SIZE, Q_ROWS + TOK_ROW + PAD, HEAD_WIDTH), got)
    pay, o_far = lax.optimization_barrier((pay, o_far))
    o_own = jnp.stack([o_own, o_far])
    got = exchange(pay, "zh")

    start = near * TOK_NEAR
    first = start + far * TOK_ROW
    cos, sin = jnp.asarray(COS_TABLE), jnp.asarray(SIN_TABLE)
    pay, new_own = run(
        rope_kernel,
        (shape(NEAR_SIZE, Q_ROWS, HEAD_WIDTH), shape(TOK_ROW, HEAD_WIDTH)),
        got,
        lax.dynamic_slice_in_dim(cos, start, TOK_NEAR),
        lax.dynamic_slice_in_dim(sin, start, TOK_NEAR),
        lax.dynamic_slice_in_dim(cos, first, TOK_ROW),
        lax.dynamic_slice_in_dim(sin, first, TOK_ROW),
        scalars=place(far, core),
    )
    new_swap = trade(new_own, "core")
    o_swap = trade(o_own, "core")
    queries = exchange(pay, "zl")
    pay = run(
        attend_kernel,
        shape(NEAR_SIZE, Q_ROWS + PAD, HEAD_WIDTH),
        queries, kv_own, kv_far, new_own, new_swap,
        scalars=place(first, core),
    )
    pay, o_swap = lax.optimization_barrier((pay, o_swap))
    got = exchange(pay, "zl")
    got = lax.all_gather(run(mix_near_kernel, shape(Q_ROWS + PAD, HEAD_WIDTH), got), "zh", axis=0)
    got = run(mix_far_kernel, shape(2 * NEAR_SIZE, Q_ROWS // 2, HEAD_WIDTH), got)
    got = exchange(got, ("zl", "core"))
    pay = run(
        output_kernel,
        shape(CHIPS, BLOCK_TOKENS // COLS, w_out.shape[1]),
        got, o_own, o_swap,
        scratch=[pltpu.VMEM((2, BLOCK_TOKENS // 2, HEAD_COLS), bf16)],
        scalars=place(mine, core),
    )
    got = exchange(pay, PLANE)
    return jnp.sum(got.astype(f32), axis=0).astype(bf16)


def solution(mesh):
    fine = Mesh(mesh.devices.reshape(2, 4, 4, 2, 4, 2), ("ylo", "zh", "zl", "yhi", "x", "core"))
    row = ("ylo", "zh", "zl")
    col = ("yhi", "x", "core")
    placed = (
        P(col, row),
        P(row),
        P(row, col),
        P(row, None),
        P(row, None),
        P(col, row),
        P(row, None),
        P(row, None),
    )
    return jax.shard_map(
        body, mesh=fine, in_specs=placed, out_specs=P(col, row), check_vma=False
    )
```

```python
import math

import jax
import jax.numpy as jnp
import numpy as np
from jax import lax
from jax.experimental import pallas as pl
from jax.experimental.pallas import tpu as pltpu
from jax.sharding import Mesh, PartitionSpec as P

MODEL_WIDTH = 8192
QUERY_HEADS = 64
KEY_VALUE_HEADS = 8
HEAD_WIDTH = 128
BLOCK_TOKENS = 512
CACHED_COUNT = 65536

rope_base = 500000.0
epsilon = 1e-05

NEAR_SIZE = 4
FAR_SIZE = 4
COLS = 16
PAIR = 2
CHIPS = 16
PLANE = ("ylo", "yhi", "x")
HEADS_HERE = QUERY_HEADS // COLS // PAIR
HEAD_COLS = HEADS_HERE * HEAD_WIDTH
TOK_NEAR = BLOCK_TOKENS // NEAR_SIZE
TOK_ROW = TOK_NEAR // FAR_SIZE
Q_ROWS = HEADS_HERE * TOK_NEAR

bf16 = jnp.bfloat16
f32 = jnp.float32


def rope_tables():
    half = HEAD_WIDTH // 2
    ladder = np.arange(half, dtype=np.float32) * np.float32(2.0 / HEAD_WIDTH)
    base = np.power(np.float32(rope_base), -ladder).astype(np.float32)
    wavelen = (np.float32(2.0 * math.pi) / base).astype(np.float32)
    smooth = ((np.float32(8192.0) / wavelen - 1) / 3).astype(np.float32)
    middle = ((1 - smooth) * base / 8 + smooth * base).astype(np.float32)
    freqs = np.where(wavelen < 2048, base, np.where(wavelen > 8192, base / 8, middle))
    pos = (CACHED_COUNT + np.arange(BLOCK_TOKENS)).astype(np.float32)
    angles = (pos[:, None] * freqs.astype(np.float32)[None, :]).astype(np.float32)
    cos = np.cos(angles.astype(np.float64)).astype(np.float32)
    sin = np.sin(angles.astype(np.float64)).astype(np.float32)
    return np.concatenate([cos, cos], 1), np.concatenate([-sin, sin], 1)


COS_TABLE, SIN_TABLE = rope_tables()


SCORE_SCALE = math.log2(math.e) / math.sqrt(HEAD_WIDTH)
LN2 = math.log(2.0)
PAD = 16
PANEL = 256


def exchange(x, axes):
    return lax.all_to_all(x, axes, 0, 0, tiled=True)


def run(kernel, shapes, *args, scratch=(), scalars=()):
    spec = pl.BlockSpec(memory_space=pltpu.VMEM)
    smem = pl.BlockSpec(memory_space=pltpu.SMEM)
    return pl.pallas_call(
        kernel,
        out_shape=shapes,
        in_specs=[smem] * len(scalars) + [spec] * len(args),
        out_specs=jax.tree.map(lambda _: spec, shapes),
        scratch_shapes=scratch,
        compiler_params=pltpu.CompilerParams(vmem_limit_bytes=48 << 20),
    )(*scalars, *args)


def shape(*dims, dtype=bf16):
    return jax.ShapeDtypeStruct(dims, dtype)


def parts3(x):
    hi = x.astype(bf16)
    rest = x - hi.astype(f32)
    mid = rest.astype(bf16)
    low = (rest - mid.astype(f32)).astype(bf16)
    return hi.astype(f32), mid.astype(f32), low.astype(f32)


def pack_rows(rows):
    line = lax.broadcasted_iota(jnp.int32, (PAD, HEAD_WIDTH), 0)
    tile = jnp.zeros((PAD, HEAD_WIDTH), f32)
    for i, row in enumerate(rows):
        tile = jnp.where(line == i, jnp.broadcast_to(row, tile.shape), tile)
    return tile.astype(bf16)


def same(rows, cols, offset=0):
    a = lax.broadcasted_iota(jnp.int32, (rows, cols), 0)
    b = lax.broadcasted_iota(jnp.int32, (rows, cols), 1)
    return a + offset == b


def to_column(row, rows, offset=0):
    wide = jnp.broadcast_to(row, (rows, row.shape[1]))
    return jnp.sum(jnp.where(same(rows, row.shape[1], offset), wide, 0.0), axis=1, keepdims=True)


def to_row(column):
    n = column.shape[0]
    wide = jnp.broadcast_to(column, (n, n))
    return jnp.sum(jnp.where(same(n, n), wide, 0.0), axis=0, keepdims=True)


def copies_kernel(x_ref, out_ref):
    for i in range(CHIPS):
        out_ref[i] = x_ref[...]


def project_kernel(pair_ref, tok_ref, gain_ref, w_ref, kv_ref, far_ref, out_ref):
    mine = pair_ref[0]
    gains = [gain_ref[...], far_ref[PANEL : PANEL + 1, :PANEL]]
    toks = []
    for side in (mine, 1 - mine):
        blocks = [tok_ref[core, side, j] for j in range(CHIPS // PAIR) for core in range(2)]
        toks.append(jnp.concatenate(blocks, axis=0))
    scaled = [(t.astype(f32) * g.astype(f32)).astype(bf16) for t, g in zip(toks, gains)]
    panels = [w_ref[...], kv_ref[...]]
    for i, panel in enumerate(panels):
        width = panel.shape[1]
        other = far_ref[:PANEL, HEAD_COLS * i : HEAD_COLS * i + width]
        part = jnp.dot(scaled[0], panel, preferred_element_type=f32)
        part = (part + jnp.dot(scaled[1], other, preferred_element_type=f32)).astype(bf16)
        for j in range(width // HEAD_WIDTH):
            head = part[:, HEAD_WIDTH * j : HEAD_WIDTH * (j + 1)]
            row = (2 * i + j) * TOK_NEAR
            for n in range(NEAR_SIZE):
                out_ref[n, row : row + TOK_NEAR, :] = head[n * TOK_NEAR : (n + 1) * TOK_NEAR]
    row = Q_ROWS + TOK_NEAR
    contract = (((1,), (1,)), ((), ()))
    for n in range(NEAR_SIZE):
        sums = jnp.zeros((1, TOK_NEAR), f32)
        for t in toks:
            x = t[n * TOK_NEAR : (n + 1) * TOK_NEAR]
            gram = lax.dot_general(x, x, contract, preferred_element_type=f32)
            gram = jnp.where(same(TOK_NEAR, TOK_NEAR), gram, 0.0)
            sums = sums + jnp.sum(gram, axis=0, keepdims=True)
        out_ref[n, row : row + PAD, :] = pack_rows(parts3(sums))


def reduce_kernel(got_ref, out_ref):
    total = got_ref[0].astype(f32)
    for n in range(1, NEAR_SIZE):
        total = total + got_ref[n].astype(f32)
    low = total.astype(bf16)
    s_row = Q_ROWS + TOK_NEAR
    sums = total[s_row : s_row + 1] + total[s_row + 1 : s_row + 2] + total[s_row + 2 : s_row + 3]
    out_ref[:s_row, :] = low[:s_row]
    out_ref[s_row:, :] = pack_rows(parts3(sums))


def rope_kernel(place_ref, got_ref, cos_ref, sin_ref, cosn_ref, sinn_ref, q_ref, new_ref):
    def gather(rows):
        total = got_ref[0, rows, :].astype(f32)
        for n in range(1, FAR_SIZE):
            total = total + got_ref[n, rows, :].astype(f32)
        return total

    tile = gather(slice(Q_ROWS + TOK_NEAR, Q_ROWS + TOK_NEAR + PAD))
    sums = tile[0:1] + tile[1:2] + tile[2:3]
    inv = lax.rsqrt(sums / MODEL_WIDTH + epsilon)
    inv_q = to_column(inv, TOK_NEAR)
    inv_n = to_column(inv, TOK_ROW, place_ref[0] * TOK_ROW)
    cos, sin = cos_ref[...], sin_ref[...]
    for h in range(HEADS_HERE):
        u = gather(slice(h * TOK_NEAR, (h + 1) * TOK_NEAR)) * inv_q
        u = (u * cos + pltpu.roll(u, HEAD_WIDTH // 2, 1) * sin).astype(bf16)
        for n in range(NEAR_SIZE):
            q_ref[n, h * TOK_NEAR : (h + 1) * TOK_NEAR, :] = u
    u = gather(pl.ds(pl.multiple_of(Q_ROWS + place_ref[0] * TOK_ROW, TOK_ROW), TOK_ROW)) * inv_n
    turned = u * cosn_ref[...] + pltpu.roll(u, HEAD_WIDTH // 2, 1) * sinn_ref[...]
    new_ref[...] = jnp.where(place_ref[1] == 0, turned, u).astype(bf16)


def attend_kernel(place_ref, q_ref, kv_ref, other_ref, own_ref, swap_ref, out_ref):
    contract = (((1,), (1,)), ((), ()))
    zeros = jnp.zeros((HEAD_WIDTH - TOK_ROW, HEAD_WIDTH), bf16)
    even = place_ref[1] == 0
    own, swap = own_ref[...].astype(f32), swap_ref[...].astype(f32)
    new_k = jnp.concatenate([jnp.where(even, own, swap).astype(bf16), zeros], axis=0)
    new_v = jnp.concatenate([jnp.where(even, swap, own).astype(bf16), zeros], axis=0)
    rows = 2 * Q_ROWS
    slot = lax.broadcasted_iota(jnp.int32, (rows, HEAD_WIDTH), 1)
    line = lax.broadcasted_iota(jnp.int32, (rows, HEAD_WIDTH), 0)
    new_token = jnp.where(slot < TOK_ROW, place_ref[0] + slot, BLOCK_TOKENS)
    at = jnp.where(line < Q_ROWS, 0, TOK_NEAR) + lax.rem(line, TOK_NEAR)
    for n in range(0, NEAR_SIZE, 2):
        q = jnp.concatenate([q_ref[n], q_ref[n + 1]], axis=0)
        top = denom = numer = None
        for k, v in ((kv_ref[0], kv_ref[1]), (other_ref[0], other_ref[1]), (new_k, new_v)):
            s = lax.dot_general(q, k, contract, preferred_element_type=f32)
            if k is new_k:
                s = jnp.where(new_token <= n * TOK_NEAR + at, s, -jnp.inf)
            here = jnp.max(s, axis=1, keepdims=True)
            most = here if top is None else jnp.maximum(top, here)
            w = jnp.exp2(s * SCORE_SCALE - most * SCORE_SCALE)
            total = jnp.sum(w, axis=1, keepdims=True)
            part = jnp.dot(w.astype(bf16), v, preferred_element_type=f32)
            if top is not None:
                fade = jnp.exp2((top - most) * SCORE_SCALE)
                total = denom * fade + total
                part = numer * fade + part
            top, denom, numer = most, total, part
        out = (numer / denom).astype(bf16)
        lse = top * (SCORE_SCALE * LN2) + jnp.log(denom)
        for i in range(2):
            out_ref[n + i, :Q_ROWS, :] = out[i * Q_ROWS : (i + 1) * Q_ROWS]
            row = i * Q_ROWS
            lo = parts3(to_row(lse[row : row + HEAD_WIDTH]))
            hi = parts3(to_row(lse[row + HEAD_WIDTH : row + Q_ROWS]))
            out_ref[n + i, Q_ROWS:, :] = pack_rows([x for pair in zip(lo, hi) for x in pair])


def mix(got_ref, count):
    lse = []
    for n in range(count):
        t = got_ref[n, Q_ROWS:, :].astype(f32)
        lse.append(t[0:2] + t[2:4] + t[4:6])
    top = lse[0]
    for n in range(1, count):
        top = jnp.maximum(top, lse[n])
    share = [jnp.exp(x - top) for x in lse]
    total = sum(share[1:], share[0])
    halves = []
    for j in range(2):
        rows = slice(HEAD_WIDTH * j, HEAD_WIDTH * (j + 1))
        acc = jnp.zeros((HEAD_WIDTH, HEAD_WIDTH), f32)
        for n in range(count):
            ratio = to_column(share[n][j : j + 1] / total[j : j + 1], HEAD_WIDTH)
            acc = acc + got_ref[n, rows, :].astype(f32) * ratio
        halves.append(acc.astype(bf16))
    return halves, top + jnp.log(total)


def mix_near_kernel(got_ref, out_ref):
    halves, lse = mix(got_ref, NEAR_SIZE)
    parts = parts3(lse)
    tile = pack_rows([p[j : j + 1] for p in parts for j in range(2)])
    out_ref[:HEAD_WIDTH, :] = halves[0]
    out_ref[HEAD_WIDTH:Q_ROWS, :] = halves[1]
    out_ref[Q_ROWS:, :] = tile


def mix_far_kernel(got_ref, out_ref):
    halves, _ = mix(got_ref, FAR_SIZE)
    rows = BLOCK_TOKENS // COLS
    for n in range(NEAR_SIZE):
        for core in range(2):
            for h in range(HEADS_HERE):
                for sub in range(2):
                    at = (2 * sub + core) * rows
                    to = (2 * h + sub) * rows
                    out_ref[2 * n + core, to : to + rows, :] = halves[h][at : at + rows]


def output_kernel(place_ref, got_ref, own_ref, swap_ref, out_ref, ctx_ref):
    mine, core = place_ref[0], place_ref[1]
    rows = BLOCK_TOKENS // COLS
    for n in range(NEAR_SIZE):
        for h in range(HEADS_HERE):
            to = slice(2 * n * rows, 2 * (n + 1) * rows)
            at = slice(2 * h * rows, 2 * (h + 1) * rows)
            lanes = slice(h * HEAD_WIDTH, (h + 1) * HEAD_WIDTH)
            ctx_ref[0, to, lanes] = got_ref[2 * n + core, at, :]
            ctx_ref[1, to, lanes] = got_ref[2 * n + 1 - core, at, :]
    for i, side in enumerate((mine, 1 - mine)):
        part = jnp.dot(ctx_ref[0], own_ref[i], preferred_element_type=f32)
        part = part + jnp.dot(ctx_ref[1], swap_ref[i], preferred_element_type=f32)
        part = part.astype(bf16)
        for c in range(CHIPS // PAIR):
            out_ref[side * (CHIPS // PAIR) + c] = part[c * rows : (c + 1) * rows]


def trade(x, axis):
    return lax.ppermute(x, axis, [(0, 1), (1, 0)])


def body(tokens, norm_gain, w_query, key_weight, value_weight, w_out, cached_keys, cached_values):
    mine = lax.axis_index("ylo")
    near = lax.axis_index("zl")
    far = lax.axis_index("zh")
    core = lax.axis_index("core")
    group = lax.axis_index("yhi") * 4 + lax.axis_index("x")

    def panel(x):
        return lax.dynamic_slice_in_dim(x, group * HEAD_WIDTH, HEAD_WIDTH, 1)

    def place(*xs):
        return (jnp.stack(xs).astype(jnp.int32),)

    kv_panel = jnp.where(core == 0, panel(key_weight), panel(value_weight))
    w_own = lax.dynamic_slice_in_dim(w_query, mine * HEAD_COLS, HEAD_COLS, 1)
    w_far = lax.dynamic_slice_in_dim(w_query, (1 - mine) * HEAD_COLS, HEAD_COLS, 1)
    w_far = jnp.concatenate([w_far, kv_panel], axis=1)
    gain_row = jnp.pad(norm_gain[None], ((0, PAD - 1), (0, w_far.shape[1] - norm_gain.shape[0])))
    w_far = trade(jnp.concatenate([w_far, gain_row], axis=0), "ylo")
    whole = lax.all_gather(exchange(run(copies_kernel, shape(CHIPS, *tokens.shape), tokens), PLANE), "core", axis=0)
    whole = whole.reshape((2, PAIR, CHIPS // PAIR) + tokens.shape)
    pay = run(
        project_kernel,
        shape(NEAR_SIZE, Q_ROWS + TOK_NEAR + PAD, HEAD_WIDTH),
        whole, norm_gain[None], w_own, kv_panel, w_far,
        scalars=place(mine),
    )
    pay, group = lax.optimization_barrier((pay, group))
    kv_own = jnp.stack([panel(cached_keys), panel(cached_values)])
    kv_far = trade(kv_own, "ylo")
    got = exchange(pay, "zl")
    pay = run(reduce_kernel, shape(Q_ROWS + TOK_NEAR + PAD, HEAD_WIDTH), got)
    got = lax.all_gather(pay, "zh", axis=0)
    got, w_out = lax.optimization_barrier((got, w_out))
    o_own = lax.dynamic_slice_in_dim(w_out, mine * HEAD_COLS, HEAD_COLS, 0)
    o_far = trade(lax.dynamic_slice_in_dim(w_out, (1 - mine) * HEAD_COLS, HEAD_COLS, 0), "ylo")

    start = near * TOK_NEAR
    first = start + far * TOK_ROW
    cos, sin = jnp.asarray(COS_TABLE), jnp.asarray(SIN_TABLE)
    pay, new_own = run(
        rope_kernel,
        (shape(NEAR_SIZE, Q_ROWS, HEAD_WIDTH), shape(TOK_ROW, HEAD_WIDTH)),
        got,
        lax.dynamic_slice_in_dim(cos, start, TOK_NEAR),
        lax.dynamic_slice_in_dim(sin, start, TOK_NEAR),
        lax.dynamic_slice_in_dim(cos, first, TOK_ROW),
        lax.dynamic_slice_in_dim(sin, first, TOK_ROW),
        scalars=place(far, core),
    )
    new_swap = trade(new_own, "core")
    queries = exchange(pay, "zl")
    pay = run(
        attend_kernel,
        shape(NEAR_SIZE, Q_ROWS + PAD, HEAD_WIDTH),
        queries, kv_own, kv_far, new_own, new_swap,
        scalars=place(first, core),
    )
    pay, o_own, o_far = lax.optimization_barrier((pay, o_own, o_far))
    got = exchange(pay, "zl")
    got = lax.all_gather(run(mix_near_kernel, shape(Q_ROWS + PAD, HEAD_WIDTH), got), "zh", axis=0)
    got = run(mix_far_kernel, shape(2 * NEAR_SIZE, Q_ROWS // 2, HEAD_WIDTH), got)
    got, o_own, o_far = lax.optimization_barrier((got, o_own, o_far))
    o_own = jnp.stack([o_own, o_far])
    o_swap = trade(o_own, "core")
    got = exchange(got, ("zl", "core"))
    pay = run(
        output_kernel,
        shape(CHIPS, BLOCK_TOKENS // COLS, w_out.shape[1]),
        got, o_own, o_swap,
        scratch=[pltpu.VMEM((2, BLOCK_TOKENS // 2, HEAD_COLS), bf16)],
        scalars=place(mine, core),
    )
    got = exchange(pay, PLANE)
    return jnp.sum(got.astype(f32), axis=0).astype(bf16)


def solution(mesh):
    fine = Mesh(mesh.devices.reshape(2, 4, 4, 2, 4, 2), ("ylo", "zh", "zl", "yhi", "x", "core"))
    row = ("ylo", "zh", "zl")
    col = ("yhi", "x", "core")
    placed = (
        P(col, row),
        P(row),
        P(row, col),
        P(row, None),
        P(row, None),
        P(col, row),
        P(row, None),
        P(row, None),
    )
    return jax.shard_map(
        body, mesh=fine, in_specs=placed, out_specs=P(col, row), check_vma=False
    )
```

```python
import math

import jax
import jax.numpy as jnp
import numpy as np
from jax import lax
from jax.experimental import pallas as pl
from jax.experimental.pallas import tpu as pltpu
from jax.sharding import Mesh, PartitionSpec as P

MODEL_WIDTH = 8192
QUERY_HEADS = 64
KEY_VALUE_HEADS = 8
HEAD_WIDTH = 128
BLOCK_TOKENS = 512
CACHED_COUNT = 65536

rope_base = 500000.0
epsilon = 1e-05

NEAR_SIZE = 4
FAR_SIZE = 4
COLS = 16
PAIR = 2
CHIPS = 16
PLANE = ("ylo", "yhi", "x")
HEADS_HERE = QUERY_HEADS // COLS // PAIR
HEAD_COLS = HEADS_HERE * HEAD_WIDTH
TOK_NEAR = BLOCK_TOKENS // NEAR_SIZE
TOK_ROW = TOK_NEAR // FAR_SIZE
Q_ROWS = HEADS_HERE * TOK_NEAR

bf16 = jnp.bfloat16
f32 = jnp.float32


def rope_tables():
    half = HEAD_WIDTH // 2
    ladder = np.arange(half, dtype=np.float32) * np.float32(2.0 / HEAD_WIDTH)
    base = np.power(np.float32(rope_base), -ladder).astype(np.float32)
    wavelen = (np.float32(2.0 * math.pi) / base).astype(np.float32)
    smooth = ((np.float32(8192.0) / wavelen - 1) / 3).astype(np.float32)
    middle = ((1 - smooth) * base / 8 + smooth * base).astype(np.float32)
    freqs = np.where(wavelen < 2048, base, np.where(wavelen > 8192, base / 8, middle))
    pos = (CACHED_COUNT + np.arange(BLOCK_TOKENS)).astype(np.float32)
    angles = (pos[:, None] * freqs.astype(np.float32)[None, :]).astype(np.float32)
    cos = np.cos(angles.astype(np.float64)).astype(np.float32)
    sin = np.sin(angles.astype(np.float64)).astype(np.float32)
    return np.concatenate([cos, cos], 1), np.concatenate([-sin, sin], 1)


COS_TABLE, SIN_TABLE = rope_tables()


SCORE_SCALE = math.log2(math.e) / math.sqrt(HEAD_WIDTH)
LN2 = math.log(2.0)
PAD = 16
PANEL = 256


def exchange(x, axes):
    return lax.all_to_all(x, axes, 0, 0, tiled=True)


def run(kernel, shapes, *args, scratch=(), scalars=()):
    spec = pl.BlockSpec(memory_space=pltpu.VMEM)
    smem = pl.BlockSpec(memory_space=pltpu.SMEM)
    return pl.pallas_call(
        kernel,
        out_shape=shapes,
        in_specs=[smem] * len(scalars) + [spec] * len(args),
        out_specs=jax.tree.map(lambda _: spec, shapes),
        scratch_shapes=scratch,
        compiler_params=pltpu.CompilerParams(vmem_limit_bytes=48 << 20),
    )(*scalars, *args)


def shape(*dims, dtype=bf16):
    return jax.ShapeDtypeStruct(dims, dtype)


def parts3(x):
    hi = x.astype(bf16)
    rest = x - hi.astype(f32)
    mid = rest.astype(bf16)
    low = (rest - mid.astype(f32)).astype(bf16)
    return hi.astype(f32), mid.astype(f32), low.astype(f32)


def pack_rows(rows):
    line = lax.broadcasted_iota(jnp.int32, (PAD, HEAD_WIDTH), 0)
    tile = jnp.zeros((PAD, HEAD_WIDTH), f32)
    for i, row in enumerate(rows):
        tile = jnp.where(line == i, jnp.broadcast_to(row, tile.shape), tile)
    return tile.astype(bf16)


def same(rows, cols, offset=0):
    a = lax.broadcasted_iota(jnp.int32, (rows, cols), 0)
    b = lax.broadcasted_iota(jnp.int32, (rows, cols), 1)
    return a + offset == b


def to_column(row, rows, offset=0):
    wide = jnp.broadcast_to(row, (rows, row.shape[1]))
    return jnp.sum(jnp.where(same(rows, row.shape[1], offset), wide, 0.0), axis=1, keepdims=True)


def to_row(column):
    n = column.shape[0]
    wide = jnp.broadcast_to(column, (n, n))
    return jnp.sum(jnp.where(same(n, n), wide, 0.0), axis=0, keepdims=True)


def copies_kernel(x_ref, out_ref):
    for i in range(CHIPS):
        out_ref[i] = x_ref[...]


def ordered(tok_ref, side):
    blocks = [tok_ref[core, side, j] for j in range(CHIPS // PAIR) for core in range(2)]
    return jnp.concatenate(blocks, axis=0)


def own_kernel(pair_ref, tok_ref, gain_ref, w_ref, kv_ref, acc_ref, sums_ref):
    mine = pair_ref[0]
    toks = [ordered(tok_ref, mine), ordered(tok_ref, 1 - mine)]
    scaled = (toks[0].astype(f32) * gain_ref[...].astype(f32)).astype(bf16)
    acc_ref[:, :HEAD_COLS] = jnp.dot(scaled, w_ref[...], preferred_element_type=f32)
    acc_ref[:, HEAD_COLS:] = jnp.dot(scaled, kv_ref[...], preferred_element_type=f32)
    contract = (((1,), (1,)), ((), ()))
    for n in range(NEAR_SIZE):
        sums = jnp.zeros((1, TOK_NEAR), f32)
        for t in toks:
            x = t[n * TOK_NEAR : (n + 1) * TOK_NEAR]
            gram = lax.dot_general(x, x, contract, preferred_element_type=f32)
            gram = jnp.where(same(TOK_NEAR, TOK_NEAR), gram, 0.0)
            sums = sums + jnp.sum(gram, axis=0, keepdims=True)
        sums_ref[n] = pack_rows(parts3(sums))


def project_kernel(pair_ref, tok_ref, far_ref, acc_ref, sums_ref, out_ref):
    gain = far_ref[PANEL : PANEL + 1, :PANEL].astype(f32)
    scaled = (ordered(tok_ref, 1 - pair_ref[0]).astype(f32) * gain).astype(bf16)
    for i, width in enumerate((HEAD_COLS, HEAD_WIDTH)):
        lanes = slice(HEAD_COLS * i, HEAD_COLS * i + width)
        part = jnp.dot(scaled, far_ref[:PANEL, lanes], preferred_element_type=f32)
        part = (acc_ref[:, lanes] + part).astype(bf16)
        for j in range(width // HEAD_WIDTH):
            head = part[:, HEAD_WIDTH * j : HEAD_WIDTH * (j + 1)]
            row = (2 * i + j) * TOK_NEAR
            for n in range(NEAR_SIZE):
                out_ref[n, row : row + TOK_NEAR, :] = head[n * TOK_NEAR : (n + 1) * TOK_NEAR]
    row = Q_ROWS + TOK_NEAR
    for n in range(NEAR_SIZE):
        out_ref[n, row : row + PAD, :] = sums_ref[n]


def reduce_kernel(got_ref, out_ref):
    total = got_ref[0].astype(f32)
    for n in range(1, NEAR_SIZE):
        total = total + got_ref[n].astype(f32)
    low = total.astype(bf16)
    s_row = Q_ROWS + TOK_NEAR
    sums = total[s_row : s_row + 1] + total[s_row + 1 : s_row + 2] + total[s_row + 2 : s_row + 3]
    out_ref[:s_row, :] = low[:s_row]
    out_ref[s_row:, :] = pack_rows(parts3(sums))


def rope_kernel(place_ref, got_ref, cos_ref, sin_ref, cosn_ref, sinn_ref, q_ref, new_ref):
    def gather(rows):
        total = got_ref[0, rows, :].astype(f32)
        for n in range(1, FAR_SIZE):
            total = total + got_ref[n, rows, :].astype(f32)
        return total

    tile = gather(slice(Q_ROWS + TOK_NEAR, Q_ROWS + TOK_NEAR + PAD))
    sums = tile[0:1] + tile[1:2] + tile[2:3]
    inv = lax.rsqrt(sums / MODEL_WIDTH + epsilon)
    inv_q = to_column(inv, TOK_NEAR)
    inv_n = to_column(inv, TOK_ROW, place_ref[0] * TOK_ROW)
    cos, sin = cos_ref[...], sin_ref[...]
    for h in range(HEADS_HERE):
        u = gather(slice(h * TOK_NEAR, (h + 1) * TOK_NEAR)) * inv_q
        u = (u * cos + pltpu.roll(u, HEAD_WIDTH // 2, 1) * sin).astype(bf16)
        for n in range(NEAR_SIZE):
            q_ref[n, h * TOK_NEAR : (h + 1) * TOK_NEAR, :] = u
    u = gather(pl.ds(pl.multiple_of(Q_ROWS + place_ref[0] * TOK_ROW, TOK_ROW), TOK_ROW)) * inv_n
    turned = u * cosn_ref[...] + pltpu.roll(u, HEAD_WIDTH // 2, 1) * sinn_ref[...]
    new_ref[...] = jnp.where(place_ref[1] == 0, turned, u).astype(bf16)


def attend_kernel(place_ref, q_ref, kv_ref, other_ref, own_ref, swap_ref, out_ref):
    contract = (((1,), (1,)), ((), ()))
    zeros = jnp.zeros((HEAD_WIDTH - TOK_ROW, HEAD_WIDTH), bf16)
    even = place_ref[1] == 0
    own, swap = own_ref[...].astype(f32), swap_ref[...].astype(f32)
    new_k = jnp.concatenate([jnp.where(even, own, swap).astype(bf16), zeros], axis=0)
    new_v = jnp.concatenate([jnp.where(even, swap, own).astype(bf16), zeros], axis=0)
    rows = 2 * Q_ROWS
    slot = lax.broadcasted_iota(jnp.int32, (rows, HEAD_WIDTH), 1)
    line = lax.broadcasted_iota(jnp.int32, (rows, HEAD_WIDTH), 0)
    new_token = jnp.where(slot < TOK_ROW, place_ref[0] + slot, BLOCK_TOKENS)
    at = jnp.where(line < Q_ROWS, 0, TOK_NEAR) + lax.rem(line, TOK_NEAR)
    for n in range(0, NEAR_SIZE, 2):
        q = jnp.concatenate([q_ref[n], q_ref[n + 1]], axis=0)
        top = denom = numer = None
        for k, v in ((kv_ref[0], kv_ref[1]), (other_ref[0], other_ref[1]), (new_k, new_v)):
            s = lax.dot_general(q, k, contract, preferred_element_type=f32)
            if k is new_k:
                s = jnp.where(new_token <= n * TOK_NEAR + at, s, -jnp.inf)
            here = jnp.max(s, axis=1, keepdims=True)
            most = here if top is None else jnp.maximum(top, here)
            w = jnp.exp2(s * SCORE_SCALE - most * SCORE_SCALE)
            total = jnp.sum(w, axis=1, keepdims=True)
            part = jnp.dot(w.astype(bf16), v, preferred_element_type=f32)
            if top is not None:
                fade = jnp.exp2((top - most) * SCORE_SCALE)
                total = denom * fade + total
                part = numer * fade + part
            top, denom, numer = most, total, part
        out = (numer / denom).astype(bf16)
        lse = top * (SCORE_SCALE * LN2) + jnp.log(denom)
        for i in range(2):
            out_ref[n + i, :Q_ROWS, :] = out[i * Q_ROWS : (i + 1) * Q_ROWS]
            row = i * Q_ROWS
            lo = parts3(to_row(lse[row : row + HEAD_WIDTH]))
            hi = parts3(to_row(lse[row + HEAD_WIDTH : row + Q_ROWS]))
            out_ref[n + i, Q_ROWS:, :] = pack_rows([x for pair in zip(lo, hi) for x in pair])


def mix(got_ref, count):
    lse = []
    for n in range(count):
        t = got_ref[n, Q_ROWS:, :].astype(f32)
        lse.append(t[0:2] + t[2:4] + t[4:6])
    top = lse[0]
    for n in range(1, count):
        top = jnp.maximum(top, lse[n])
    share = [jnp.exp(x - top) for x in lse]
    total = sum(share[1:], share[0])
    halves = []
    for j in range(2):
        rows = slice(HEAD_WIDTH * j, HEAD_WIDTH * (j + 1))
        acc = jnp.zeros((HEAD_WIDTH, HEAD_WIDTH), f32)
        for n in range(count):
            ratio = to_column(share[n][j : j + 1] / total[j : j + 1], HEAD_WIDTH)
            acc = acc + got_ref[n, rows, :].astype(f32) * ratio
        halves.append(acc.astype(bf16))
    return halves, top + jnp.log(total)


def mix_near_kernel(got_ref, out_ref):
    halves, lse = mix(got_ref, NEAR_SIZE)
    parts = parts3(lse)
    tile = pack_rows([p[j : j + 1] for p in parts for j in range(2)])
    out_ref[:HEAD_WIDTH, :] = halves[0]
    out_ref[HEAD_WIDTH:Q_ROWS, :] = halves[1]
    out_ref[Q_ROWS:, :] = tile


def mix_far_kernel(got_ref, out_ref):
    halves, _ = mix(got_ref, FAR_SIZE)
    rows = BLOCK_TOKENS // COLS
    for n in range(NEAR_SIZE):
        for core in range(2):
            for h in range(HEADS_HERE):
                for sub in range(2):
                    at = (2 * sub + core) * rows
                    to = (2 * h + sub) * rows
                    out_ref[2 * n + core, to : to + rows, :] = halves[h][at : at + rows]


def output_kernel(place_ref, got_ref, own_ref, swap_ref, out_ref, ctx_ref):
    mine, core = place_ref[0], place_ref[1]
    rows = BLOCK_TOKENS // COLS
    for n in range(NEAR_SIZE):
        for h in range(HEADS_HERE):
            to = slice(2 * n * rows, 2 * (n + 1) * rows)
            at = slice(2 * h * rows, 2 * (h + 1) * rows)
            lanes = slice(h * HEAD_WIDTH, (h + 1) * HEAD_WIDTH)
            ctx_ref[0, to, lanes] = got_ref[2 * n + core, at, :]
            ctx_ref[1, to, lanes] = got_ref[2 * n + 1 - core, at, :]
    for i, side in enumerate((mine, 1 - mine)):
        part = jnp.dot(ctx_ref[0], own_ref[i], preferred_element_type=f32)
        part = part + jnp.dot(ctx_ref[1], swap_ref[i], preferred_element_type=f32)
        part = part.astype(bf16)
        for c in range(CHIPS // PAIR):
            out_ref[side * (CHIPS // PAIR) + c] = part[c * rows : (c + 1) * rows]


def trade(x, axis):
    return lax.ppermute(x, axis, [(0, 1), (1, 0)])


def body(tokens, norm_gain, w_query, key_weight, value_weight, w_out, cached_keys, cached_values):
    mine = lax.axis_index("ylo")
    near = lax.axis_index("zl")
    far = lax.axis_index("zh")
    core = lax.axis_index("core")
    group = lax.axis_index("yhi") * 4 + lax.axis_index("x")

    def panel(x):
        return lax.dynamic_slice_in_dim(x, group * HEAD_WIDTH, HEAD_WIDTH, 1)

    def place(*xs):
        return (jnp.stack(xs).astype(jnp.int32),)

    kv_panel = jnp.where(core == 0, panel(key_weight), panel(value_weight))
    w_own = lax.dynamic_slice_in_dim(w_query, mine * HEAD_COLS, HEAD_COLS, 1)
    w_far = lax.dynamic_slice_in_dim(w_query, (1 - mine) * HEAD_COLS, HEAD_COLS, 1)
    w_far = jnp.concatenate([w_far, kv_panel], axis=1)
    gain_row = jnp.pad(norm_gain[None], ((0, PAD - 1), (0, w_far.shape[1] - norm_gain.shape[0])))
    w_far = trade(jnp.concatenate([w_far, gain_row], axis=0), "ylo")
    whole = lax.all_gather(exchange(run(copies_kernel, shape(CHIPS, *tokens.shape), tokens), PLANE), "core", axis=0)
    whole = whole.reshape((2, PAIR, CHIPS // PAIR) + tokens.shape)
    acc, sums = run(
        own_kernel,
        (
            shape(BLOCK_TOKENS, HEAD_COLS + HEAD_WIDTH, dtype=f32),
            shape(NEAR_SIZE, PAD, HEAD_WIDTH),
        ),
        whole, norm_gain[None], w_own, kv_panel,
        scalars=place(mine),
    )
    pay = run(
        project_kernel,
        shape(NEAR_SIZE, Q_ROWS + TOK_NEAR + PAD, HEAD_WIDTH),
        whole, w_far, acc, sums,
        scalars=place(mine),
    )
    pay, group = lax.optimization_barrier((pay, group))
    kv_own = jnp.stack([panel(cached_keys), panel(cached_values)])
    kv_far = trade(kv_own, "ylo")
    got = exchange(pay, "zl")
    pay = run(reduce_kernel, shape(Q_ROWS + TOK_NEAR + PAD, HEAD_WIDTH), got)
    got = lax.all_gather(pay, "zh", axis=0)
    got, w_out = lax.optimization_barrier((got, w_out))
    o_own = lax.dynamic_slice_in_dim(w_out, mine * HEAD_COLS, HEAD_COLS, 0)
    o_far = trade(lax.dynamic_slice_in_dim(w_out, (1 - mine) * HEAD_COLS, HEAD_COLS, 0), "ylo")

    start = near * TOK_NEAR
    first = start + far * TOK_ROW
    cos, sin = jnp.asarray(COS_TABLE), jnp.asarray(SIN_TABLE)
    pay, new_own = run(
        rope_kernel,
        (shape(NEAR_SIZE, Q_ROWS, HEAD_WIDTH), shape(TOK_ROW, HEAD_WIDTH)),
        got,
        lax.dynamic_slice_in_dim(cos, start, TOK_NEAR),
        lax.dynamic_slice_in_dim(sin, start, TOK_NEAR),
        lax.dynamic_slice_in_dim(cos, first, TOK_ROW),
        lax.dynamic_slice_in_dim(sin, first, TOK_ROW),
        scalars=place(far, core),
    )
    new_swap = trade(new_own, "core")
    queries = exchange(pay, "zl")
    pay = run(
        attend_kernel,
        shape(NEAR_SIZE, Q_ROWS + PAD, HEAD_WIDTH),
        queries, kv_own, kv_far, new_own, new_swap,
        scalars=place(first, core),
    )
    pay, o_own, o_far = lax.optimization_barrier((pay, o_own, o_far))
    got = exchange(pay, "zl")
    got = lax.all_gather(run(mix_near_kernel, shape(Q_ROWS + PAD, HEAD_WIDTH), got), "zh", axis=0)
    got = run(mix_far_kernel, shape(2 * NEAR_SIZE, Q_ROWS // 2, HEAD_WIDTH), got)
    got, o_own, o_far = lax.optimization_barrier((got, o_own, o_far))
    o_own = jnp.stack([o_own, o_far])
    o_swap = trade(o_own, "core")
    got = exchange(got, ("zl", "core"))
    pay = run(
        output_kernel,
        shape(CHIPS, BLOCK_TOKENS // COLS, w_out.shape[1]),
        got, o_own, o_swap,
        scratch=[pltpu.VMEM((2, BLOCK_TOKENS // 2, HEAD_COLS), bf16)],
        scalars=place(mine, core),
    )
    got = exchange(pay, PLANE)
    return jnp.sum(got.astype(f32), axis=0).astype(bf16)


def solution(mesh):
    fine = Mesh(mesh.devices.reshape(2, 4, 4, 2, 4, 2), ("ylo", "zh", "zl", "yhi", "x", "core"))
    row = ("ylo", "zh", "zl")
    col = ("yhi", "x", "core")
    placed = (
        P(col, row),
        P(row),
        P(row, col),
        P(row, None),
        P(row, None),
        P(col, row),
        P(row, None),
        P(row, None),
    )
    return jax.shard_map(
        body, mesh=fine, in_specs=placed, out_specs=P(col, row), check_vma=False
    )
```
